32 devices in a mesh: seq: 8 (over z, x), head: 4 (over y, core).
Axes of the slice: x: 2, y: 2, z: 4, core: 2. Of those that a mesh axis runs over, the one named last changes fastest.
Arguments:
- x_in: bfloat16 [4096, 8192], P('seq', 'head'), may hold values from -1.5 to 1.5
- z_in: bfloat16 [4096, 8192], P('seq', 'head'), may hold values from -6 to 6
- bc_in: bfloat16 [4096, 8, 2, 128], P('seq', 'head'), may hold values from -3 to 3
- dt_raw: float32 [4096, 128], P('seq', 'head'), may hold values from -4 to 1000
- dt_bias: float32 [128], P('head'), may hold values from -5 to 1.5
- a_log: float32 [128], P('head'), may hold values from -8 to -2
- conv_x: bfloat16 [4, 8192], P(None, 'head'), may hold values from -3 to 3
- conv_bc: bfloat16 [4, 8, 2, 128], P(None, 'head'), may hold values from -3 to 3
- skip_gain: float32 [128], P('head'), may hold values from 0.5 to 2
- norm_gain: bfloat16 [8192], P('head'), may hold values from 0.099609375 to 1.8984375
- score_weight: bfloat16 [8192], P('head'), may hold values from -0.25 to 0.25
- passage_ids: int32 [4096], P('seq'), may hold values from 0 to 99, as said below
- teacher_logits: float32 [100], replicated, may hold values from -12 to 12
- teacher_order: int32 [100], replicated, may hold values from 0 to 99, each once
Outputs:
- mixed_out: bfloat16 [4096, 8192], P('seq', 'head')
- token_grad: float32 [4096], P('seq')
- kl_loss: float32 [], replicated
The draws below stay inside these ranges and needn't reach their ends.
Inputs may be any that keep to these rules, and one draw needn't show every extreme that they name: `passage_ids`: never falls along the tokens; each of the 100 passages has at least one token and at most 122, and one has exactly that many. Each passage appears once; teacher_logits[r] is the teacher's logit of passage teacher_order[r].
All inputs are finite; a program needn't handle non-finite values.
Results may differ from the reference program's by a relative error of at most 0.0051.
Values may be sent and summed in bfloat16 or wider, within the bound.
No kernel may reach another device: no remote copies, remote signals or barrier semaphores. Data moves between devices by JAX's collectives and lax.ppermute only.
A program may use at most 128 MiB of HBM per device.

```python
import jax
import jax.numpy as jnp
from jax import lax

H = 128
P_SIZE = 64
N = 128
G = 8
K = 4
CH = 128
NP = 100
TOK_DEV = 512
E = 8192
TOKENS = 4096


def softplus_inverse(values):
    return values + jnp.log(-jnp.expm1(-values))


def decay_plan(key):
    base = jax.random.fold_in(key, 7)
    pick_key, fast_key, middle_key, slow_key = jax.random.split(base, 4)
    fast_share = 0.3
    slow_share = 0.2
    pick = jax.random.uniform(pick_key, (H,))
    fast = pick < fast_share
    slow = pick >= 1.0 - slow_share
    fast_span = jax.random.uniform(fast_key, (H,), minval=30.0, maxval=50.0)
    middle_span = TOK_DEV * jnp.exp(jax.random.uniform(middle_key, (H,), minval=jnp.log(0.5), maxval=jnp.log(4.0)))
    slow_span = TOKENS / jax.random.uniform(slow_key, (H,), minval=0.2, maxval=1.5)
    span = jnp.where(fast, fast_span, jnp.where(slow, slow_span, middle_span))
    step_size = 4.0 / jnp.sqrt(span)
    logarithm_coefficient = -jnp.log(span * step_size)
    shifted_bias = softplus_inverse(step_size)
    return (logarithm_coefficient, shifted_bias)


def spike_positions(key):
    return jax.random.randint(jax.random.fold_in(key, 17), (3,), 0, TOKENS)


def draw_a_log(key, part):
    logarithm_coefficient, shifted_bias = decay_plan(key)
    return logarithm_coefficient.astype(jnp.float32)


def draw_dt_bias(key, part):
    logarithm_coefficient, shifted_bias = decay_plan(key)
    return shifted_bias.astype(jnp.float32)


def draw_dt_raw(key, part):
    logarithm_coefficient, shifted_bias = decay_plan(key)
    noise_key, block_key, depth_key = jax.random.split(jax.random.fold_in(key, 13), 3)
    random_jitter = jnp.clip(0.5 * jax.random.normal(noise_key, (TOKENS, H)), -2.5, 2.5)
    offsets = jax.random.uniform(block_key, (TOKENS // TOK_DEV, H), minval=-0.7, maxval=0.7)
    random_jitter = random_jitter + jnp.repeat(offsets, TOK_DEV, axis=0)
    spike_locations = spike_positions(key)
    masked_hit = jnp.any(jnp.arange(TOKENS)[:, None] == spike_locations[None, :], axis=1)
    layer_depth = jax.random.uniform(depth_key, (TOKENS, H), minval=0.22, maxval=0.5)
    spike_amount = softplus_inverse(layer_depth * jnp.exp(-logarithm_coefficient)[None, :]) - shifted_bias[None, :]
    return jnp.where(masked_hit[:, None], spike_amount, random_jitter).astype(jnp.float32)


def draw_x_in(key, part):
    spike_locations = spike_positions(key)
    rows_index = jnp.arange(TOKENS)
    ahead = spike_locations[None, :] - rows_index[:, None]
    quiet = jnp.any((ahead >= 0) & (ahead < K), axis=1)
    values = jnp.clip(0.25 * jax.random.normal(jax.random.fold_in(key, 19), (TOKENS, E)), -1.5, 1.5)
    return jnp.where(quiet[:, None], 0.0, values).astype(jnp.bfloat16)


def draw_teacher_logits(key, part):
    values_key = jax.random.fold_in(key, 23)
    values = jnp.clip(3.0 * jax.random.normal(values_key, (NP,)), -12.0, 12.0)
    return values.astype(jnp.float32)


def draw_passage_ids(key, part):
    pick_key, weight_key = jax.random.split(jax.random.fold_in(key, 29))
    longest = 3 * TOKENS // NP
    spare = TOKENS - longest - (NP - 1)
    labels = jnp.arange(NP, dtype=jnp.int32)
    chosen = jax.random.randint(pick_key, (), 0, NP)
    shares = jax.random.randint(weight_key, (NP,), 2, 5)
    shares = jnp.where(labels == chosen, 0, shares).astype(jnp.int32)
    running = jnp.cumsum(shares).astype(jnp.int32)
    edges = spare * running // running[-1]
    extra = edges - jnp.concatenate([jnp.zeros((1,), jnp.int32), edges[:-1]])
    lengths = jnp.where(labels == chosen, longest, 1 + extra).astype(jnp.int32)
    starts = (jnp.cumsum(lengths) - lengths).astype(jnp.int32)
    positions = jnp.arange(TOKENS, dtype=jnp.int32)
    ids = jnp.sum((positions[:, None] >= starts[None, 1:]).astype(jnp.int32), axis=1)
    return ids.astype(jnp.int32)


def levels(stream_key, shape, cuts, least, high):
    loudness, own = 1.0, jax.random.fold_in(stream_key, 6)
    for dim, parts in cuts:
        draws = jnp.exp(jax.random.uniform(jax.random.fold_in(own, dim), (parts,), jnp.float32, least / len(cuts), high / len(cuts)))
        loudness = loudness * jnp.repeat(draws, shape[dim] // parts).reshape([-1 if axis == dim else 1 for axis in range(len(shape))])
    return loudness


def centred(own_key, extent, scale, bound, shards=(), kind=jnp.bfloat16):
    result = scale * jax.random.normal(own_key, extent, jnp.float32)
    if shards:
        result = result * levels(own_key, extent, shards, -0.22, 0.18)
    return jnp.clip(result, -bound, bound).astype(kind)


def setup_inputs(seed: int = 0) -> dict:
    splits = jax.random.split(jax.random.key(seed), 15)
    return {
        "x_in": draw_x_in(jax.random.fold_in(splits[14], 71), 0),
        "z_in": centred(splits[1], (TOKENS, E), 1.0, 6.0, ((0, 8), (1, 4))),
        "bc_in": centred(splits[2], (TOKENS, G, 2, N), 0.5, 3.0, ((0, 8), (1, 4))),
        "dt_raw": draw_dt_raw(jax.random.fold_in(splits[14], 71), 0),
        "dt_bias": draw_dt_bias(jax.random.fold_in(splits[14], 71), 0),
        "a_log": draw_a_log(jax.random.fold_in(splits[14], 71), 0),
        "conv_x": centred(splits[6], (K, E), K ** -0.5, 3.0, ((1, 4),)),
        "conv_bc": centred(splits[7], (K, G, 2, N), K ** -0.5, 3.0, ((1, 4),)),
        "skip_gain": jnp.clip(0.5 + 1.5 * jax.random.uniform(splits[8], (H,), jnp.float32) ** levels(splits[8], (H,), ((0, 4),), -0.2, 0.2), 0.5, 2.0),
        "norm_gain": jnp.clip(1.0 + 0.18 * jax.random.normal(splits[9], (E,), jnp.float32), 0.099609375, 1.8984375).astype(jnp.bfloat16),
        "score_weight": centred(splits[10], (E,), 512 ** -0.5, 0.25, ((0, 4),)),
        "passage_ids": draw_passage_ids(jax.random.fold_in(splits[14], 71), 0),
        "teacher_logits": draw_teacher_logits(jax.random.fold_in(splits[14], 71), 0),
        "teacher_order": jax.random.permutation(splits[13], NP).astype(jnp.int32),
    }


EPS = 1e-05
CAP = 8.0

def convolve(padded, kernel, length):
    total = jnp.zeros((length,) + padded.shape[1:], jnp.float32)
    for tap in range(kernel.shape[0]):
        total = total + padded[tap:tap + length].astype(jnp.float32) * kernel[tap].astype(jnp.float32)
    return jax.nn.silu(total).astype(jnp.bfloat16)

def block_terms(inputs, bmat, cmat, steps, rates, per_group):
    length = inputs.shape[0]
    cumul = jnp.cumsum(rates, axis=0)
    pairs = jnp.einsum('tgn,sgn->gts', cmat.astype(jnp.float32), bmat.astype(jnp.float32))
    pairs = jnp.repeat(pairs, per_group, axis=0)
    rows = lax.broadcasted_iota(jnp.int32, (length, length), 0)
    cols = lax.broadcasted_iota(jnp.int32, (length, length), 1)
    lower = (rows >= cols)[None]
    across = cumul.T
    gap = jnp.where(lower, across[:, :, None] - across[:, None, :], 0.0)
    scale_multiplier = jnp.where(lower, jnp.exp(gap), 0.0)
    weight_values = (pairs * scale_multiplier * steps.T[:, None, :]).astype(jnp.bfloat16)
    inner = jnp.einsum('hts,shp->thp', weight_values.astype(jnp.float32), inputs.astype(jnp.float32))
    tail_scale = jnp.exp(cumul[-1][None, :] - cumul) * steps
    loaded = (inputs.astype(jnp.float32) * tail_scale[:, :, None]).astype(jnp.bfloat16)
    broadcast_heads = jnp.repeat(bmat, per_group, axis=1)
    added = jnp.einsum('shn,shp->hnp', broadcast_heads.astype(jnp.float32), loaded.astype(jnp.float32))
    return (inner, added, cumul)

def reference(x_in, z_in, bc_in, dt_raw, dt_bias, a_log, conv_x, conv_bc, skip_gain, norm_gain, score_weight, passage_ids, teacher_logits, teacher_order):
    width = conv_x.shape[0]
    per_group = H // G
    x_pad = jnp.concatenate([jnp.zeros((width - 1, H * P_SIZE), jnp.bfloat16), x_in], axis=0)
    bc_pad = jnp.concatenate([jnp.zeros((width - 1, G, 2, N), jnp.bfloat16), bc_in], axis=0)
    steps_all = jax.nn.softplus(dt_raw + dt_bias[None, :])
    every_rate = -jnp.exp(a_log)[None, :] * steps_all
    gain = norm_gain.astype(jnp.float32)

    def advance(carry, index):
        start = index * CH
        x_win = lax.dynamic_slice_in_dim(x_pad, start, CH + width - 1, 0)
        bc_win = lax.dynamic_slice_in_dim(bc_pad, start, CH + width - 1, 0)
        inputs = convolve(x_win, conv_x, CH).reshape(CH, H, P_SIZE)
        bc_conv = convolve(bc_win, conv_bc, CH)
        bmat = bc_conv[:, :, 0, :]
        cmat = bc_conv[:, :, 1, :]
        steps = lax.dynamic_slice_in_dim(steps_all, start, CH, 0)
        rates = lax.dynamic_slice_in_dim(every_rate, start, CH, 0)
        inner, added, cumul = block_terms(inputs, bmat, cmat, steps, rates, per_group)
        cheads = jnp.repeat(cmat, per_group, axis=1).astype(jnp.float32)
        outer = jnp.einsum('thn,hnp->thp', cheads, carry, precision=lax.Precision.HIGHEST)
        ssd = inner + jnp.exp(cumul)[:, :, None] * outer + skip_gain[None, :, None] * inputs.astype(jnp.float32)
        gate_part = lax.dynamic_slice_in_dim(z_in, start, CH, 0)
        gated = ssd.reshape(CH, G, per_group * P_SIZE) * jax.nn.silu(gate_part.astype(jnp.float32)).reshape(CH, G, per_group * P_SIZE)
        power = lax.optimization_barrier(jnp.mean(gated * gated, axis=2, keepdims=True))
        mixed = ((gated * lax.rsqrt(power + EPS)).reshape(CH, H * P_SIZE) * gain).astype(jnp.bfloat16)
        readout = jnp.dot(mixed, score_weight, preferred_element_type=jnp.float32)
        carry = jnp.exp(cumul[-1])[:, None, None] * carry + added
        return (carry, (mixed, readout))
    start_state = jnp.zeros((H, N, P_SIZE), jnp.float32)
    closing_state, results = lax.scan(advance, start_state, jnp.arange(x_in.shape[0] // CH, dtype=jnp.int32))
    mixed_out = results[0].reshape(-1, H * P_SIZE)
    readout = results[1].reshape(-1)
    sums = jax.ops.segment_sum(readout, passage_ids, num_segments=NP)
    counts = jax.ops.segment_sum(jnp.ones(readout.shape, jnp.float32), passage_ids, num_segments=NP)
    means = sums / counts
    squash = jnp.tanh(means / CAP)
    scores = CAP * squash
    student = scores - jnp.log(jnp.sum(jnp.exp(scores)))
    teacher = jnp.zeros((NP,), jnp.float32).at[teacher_order].set(teacher_logits)
    teacher = teacher - jnp.log(jnp.sum(jnp.exp(teacher)))
    kl_loss = jnp.sum(jnp.exp(teacher) * (teacher - student))
    coef = (jnp.exp(student) - jnp.exp(teacher)) * (1.0 - squash * squash) * TOKENS / counts
    token_grad = coef[passage_ids]
    return (mixed_out, token_grad, kl_loss)
```

```python
from functools import partial

import jax
import jax.numpy as jnp
from jax import lax
from jax.experimental import pallas as pl
from jax.experimental.pallas import tpu as pltpu
from jax.sharding import PartitionSpec as P

CH = 128
NP = 100
LANES = 128


EPS = 1e-05
CAP = 8.0

F32 = jnp.float32
BF16 = jnp.bfloat16
HIGH = lax.Precision.HIGHEST
VMEM_LIMIT = 24 * 1024 * 1024


def silu(v):
    half = 0.5 * v
    return half + half * jnp.tanh(half)


def convolved(cur, prev, taps):
    full = jnp.concatenate([prev, cur], axis=0)
    back = pltpu.roll(full, 1, 0)
    early = taps[1:2] * full + taps[0:1] * back
    late = taps[3:4] * cur + taps[2:3] * back[8:]
    return silu(late + pltpu.roll(early, 2, 0)[8:])


def split(values):
    rows, heads = values.shape
    high = values.astype(BF16).astype(F32)
    parts = [high, values - high]
    if 2 * heads < LANES:
        parts.append(jnp.zeros((rows, LANES - 2 * heads), F32))
    return jnp.concatenate(parts, axis=1).astype(BF16)


def spreader(heads, head_size):
    shape = (LANES, heads * head_size)
    row = lax.broadcasted_iota(jnp.int32, shape, 0)
    col = lax.broadcasted_iota(jnp.int32, shape, 1) // head_size
    hit = (row == col) | (row == col + heads)
    return jnp.where(hit, 1.0, 0.0).astype(BF16)


def dot(a, b, precision=None):
    return jnp.dot(a, b, preferred_element_type=F32, precision=precision)


def state_kernel(
    me_ref,
    x_ref,
    halo_ref,
    bc_ref,
    dt_ref,
    bias_ref,
    alog_ref,
    kx_ref,
    kbc_ref,
    xc_ref,
    bcc_ref,
    carry_ref,
    cum_ref,
    row_ref,
    ecs_ref,
    *rest,
    head_size,
    groups,
):
    pieces, (px, pbc, state, spread, total) = rest[:-5], rest[-5:]
    block = pl.program_id(0)
    width = x_ref.shape[1]
    heads = dt_ref.shape[1]
    span = width // groups

    @pl.when(block == 0)
    def _():
        edge = halo_ref[...].astype(F32)
        px[5:8, :] = edge[:, :width]
        pbc[5:8, :] = edge[:, width:]
        state[...] = jnp.zeros_like(state)
        total[...] = jnp.zeros_like(total)
        spread[...] = spreader(heads, head_size)

    v = dt_ref[...] + bias_ref[...]
    steps = jnp.maximum(v, 0.0) + jnp.log1p(jnp.exp(-jnp.abs(v)))
    rates = -jnp.exp(alog_ref[...]) * steps
    r = lax.broadcasted_iota(jnp.int32, (CH, CH), 0)
    c = lax.broadcasted_iota(jnp.int32, (CH, CH), 1)
    lower = jnp.where(r >= c, 1.0, 0.0)
    cum = dot(lower, rates, HIGH)
    last = cum[CH - 1 : CH, :]
    cum_ref[...] = cum
    pad = jnp.zeros((CH, LANES - heads), F32)
    gap = jnp.concatenate([cum - jnp.log(steps), pad], axis=1)
    row_ref[0] = gap.T[:heads, :]
    ecs_ref[...] = jnp.exp(total[0:1, :heads] + cum)
    total[0:1, :heads] = total[0:1, :heads] + last
    tails = split(jnp.exp(last - cum) * steps)
    decay = split(jnp.exp(jnp.broadcast_to(last, (8, heads))))

    trans = []
    for part in range(2 * groups):
        at = slice(part * LANES, (part + 1) * LANES)
        cur = bc_ref[:, at].astype(F32)
        done = convolved(cur, pbc[:, at], kbc_ref[:, at].astype(F32))
        pbc[:, at] = cur[CH - 8 :]
        bcc_ref[:, at] = done.astype(BF16)
        if part % 2 == 0:
            trans.append(done.astype(BF16).astype(F32).T.astype(BF16))

    for group in range(groups):
        for begin in range(group * span, (group + 1) * span, 256):
            loads = []
            for start in (begin, begin + LANES):
                at = slice(start, start + LANES)
                cur = x_ref[:, at].astype(F32)
                done = convolved(cur, px[:, at], kx_ref[:, at].astype(F32)).astype(BF16)
                px[:, at] = cur[CH - 8 :]
                xc_ref[:, at] = done
                scale = dot(tails, spread[:, at])
                loads.append((done.astype(F32) * scale).astype(BF16))
            at = slice(begin, begin + 256)
            added = dot(trans[group], jnp.concatenate(loads, axis=1))
            before = state[:, at]
            carry_ref[0, :, at] = before.astype(BF16)
            state[:, at] = dot(decay, spread[:, at])[0:1] * before + added

    @pl.when(block == pl.num_programs(0) - 1)
    def _():
        size = len(pieces)
        rows = state.shape[0] // size
        final = split(jnp.exp(jnp.broadcast_to(total[0:1, :heads], (rows, heads))))
        for step, piece in enumerate(pieces):
            owner = me_ref[0] ^ step
            take = state[pl.ds(pl.multiple_of(owner * rows, rows), rows), :]
            piece[:, :width] = take.astype(BF16)
            piece[:, width:] = final


def prefix_kernel(me_ref, *rest, head_size, heads):
    size = len(rest) - 6
    pieces = rest[:size]
    part_ref, gain_ref, out_ref, states, decays, spread = rest[size:]
    rows = out_ref.shape[0]
    width = out_ref.shape[1]
    for step, piece in enumerate(pieces):
        owner = me_ref[0] ^ step
        states[owner] = piece[:, :width].astype(F32)
        decays[owner] = piece[:, width:].astype(F32)
    spread[...] = spreader(heads, head_size)
    held = jnp.zeros((rows, width), F32)
    gain = jnp.ones((1, width), F32)
    for shard in range(size):
        part_ref[shard] = held
        gain_ref[shard] = gain
        factor = dot(decays[shard].astype(BF16), spread[...])[0:1]
        held = factor * held + states[shard]
        gain = factor * gain
    out_ref[...] = held.astype(BF16)


def enter_kernel(me_ref, part_ref, gain_ref, low_ref, *outs):
    low = low_ref[...].astype(F32)
    for step, out in enumerate(outs):
        owner = me_ref[0] ^ step
        out[...] = (part_ref[owner] + gain_ref[owner] * low).astype(BF16)


def inner_kernel(
    xc_ref,
    bcc_ref,
    carry_ref,
    cum_ref,
    row_ref,
    ecs_ref,
    z_ref,
    skip_ref,
    y_ref,
    p_ref,
    spread,
    *,
    head_size,
    groups,
):
    block = pl.program_id(0)
    width = xc_ref.shape[1]
    heads = cum_ref.shape[1]
    per_group = heads // groups
    span = width // groups

    @pl.when(block == 0)
    def _():
        spread[...] = spreader(heads, head_size)

    cum = cum_ref[...]
    rowed = row_ref[0]
    grown = split(jnp.exp(cum))
    whole = split(ecs_ref[...])
    skips = split(jnp.broadcast_to(skip_ref[...], (8, heads)))
    r = lax.broadcasted_iota(jnp.int32, (CH, CH), 0)
    c = lax.broadcasted_iota(jnp.int32, (CH, CH), 1)
    left = c < head_size
    per_tile = LANES // head_size
    for group in range(groups):
        bmat = bcc_ref[:, 2 * group * LANES : (2 * group + 1) * LANES]
        cmat = bcc_ref[:, (2 * group + 1) * LANES : (2 * group + 2) * LANES]
        pairs = lax.dot_general(
            cmat, bmat, (((1,), (1,)), ((), ())), preferred_element_type=F32
        )
        pairs = jnp.where(r >= c, pairs, 0.0)
        for tile in range(span // LANES):
            at = slice(group * span + tile * LANES, group * span + (tile + 1) * LANES)
            xc = xc_ref[:, at]
            weights = []
            for k in range(per_tile):
                head = group * per_group + tile * per_tile + k
                gap = cum[:, head : head + 1] - rowed[head : head + 1, :]
                weights.append((pairs * jnp.exp(jnp.minimum(gap, 60.0))).astype(BF16))
            zero = jnp.zeros_like(xc)
            stacked = jnp.concatenate(
                [jnp.where(left, xc, zero), jnp.where(left, zero, xc)], axis=0
            )
            y = dot(jnp.concatenate(weights, axis=1), stacked)
            y = y + dot(grown, spread[:, at]) * dot(cmat, carry_ref[0, :, at])
            y = y + dot(skips, spread[:, at])[0:1] * xc.astype(F32)
            gate = silu(z_ref[:, at].astype(F32))
            y_ref[:, at] = y * gate
            p_ref[:, at] = (gate * dot(whole, spread[:, at])).astype(BF16)


def mix_kernel(me_ref, y_ref, p_ref, bcc_ref, gain_ref, weight_ref, ids_ref, *rest, groups):
    pieces = rest[:-6]
    mixed_ref, out_ref, wide, enter, gated, acc = rest[-6:]
    block = pl.program_id(0)
    width = y_ref.shape[1]
    span = width // groups
    size = len(pieces)
    rows = wide.shape[0] // size

    @pl.when(block == 0)
    def _():
        for step, piece in enumerate(pieces):
            owner = me_ref[0] ^ step
            wide[pl.ds(pl.multiple_of(owner * rows, rows), rows), :] = piece[...].astype(F32)
        enter[...] = wide[...].astype(BF16)
        acc[...] = jnp.zeros_like(acc)

    read = jnp.zeros((CH, LANES), F32)
    for group in range(groups):
        cmat = bcc_ref[:, (2 * group + 1) * LANES : (2 * group + 2) * LANES]
        square = jnp.zeros((CH, LANES), F32)
        for start in range(0, span, LANES):
            at = slice(group * span + start, group * span + start + LANES)
            g = y_ref[:, at] + p_ref[:, at].astype(F32) * dot(cmat, enter[:, at])
            gated[:, at] = g
            square = square + g * g
        scale = lax.rsqrt(jnp.sum(square, axis=1, keepdims=True) / span + EPS)
        scale = jnp.broadcast_to(scale, (CH, LANES))
        for start in range(0, span, LANES):
            at = slice(group * span + start, group * span + start + LANES)
            mixed = (gated[:, at] * scale * gain_ref[:, at].astype(F32)).astype(BF16)
            mixed_ref[:, at] = mixed
            read = read + mixed.astype(F32) * weight_ref[:, at].astype(F32)
    labels = lax.broadcasted_iota(jnp.int32, (LANES, CH), 0)
    member = jnp.where(labels == ids_ref[0], 1.0, 0.0)
    acc[0] += dot(member, read, HIGH)
    acc[1] += member

    @pl.when(block == pl.num_programs(0) - 1)
    def _():
        lane = lax.broadcasted_iota(jnp.int32, (LANES, LANES), 1)
        sums = jnp.sum(acc[0], axis=1, keepdims=True)
        counts = jnp.sum(acc[1], axis=1, keepdims=True)
        both = jnp.where(lane == 0, sums, jnp.where(lane == 1, counts, 0.0)).T
        out_ref[...] = jnp.broadcast_to(both[None, :2, :], out_ref.shape)


def loss_kernel(parts_ref, ids_ref, logits_ref, order_ref, grad_ref, loss_ref, *, copies, total):
    both = jnp.sum(parts_ref[...], axis=0)
    lane = lax.broadcasted_iota(jnp.int32, (1, LANES), 1)
    valid = lane < NP
    sums = both[0:1]
    counts = jnp.where(valid, both[1:2] / copies, 1.0)
    squash = jnp.tanh(sums / counts / CAP)
    scores = CAP * squash
    student = scores - jnp.log(jnp.sum(jnp.where(valid, jnp.exp(scores), 0.0)))
    hit = order_ref[...] == lax.broadcasted_iota(jnp.int32, (NP, LANES), 1)
    teacher = jnp.sum(jnp.where(hit, logits_ref[...], 0.0), axis=0, keepdims=True)
    teacher = teacher - jnp.log(jnp.sum(jnp.where(valid, jnp.exp(teacher), 0.0)))
    chance = jnp.where(valid, jnp.exp(teacher), 0.0)
    loss_ref[0, 0] = jnp.sum(chance * (teacher - student))
    coef = (jnp.exp(student) - chance) * (1.0 - squash * squash) * total / counts
    coef = jnp.broadcast_to(jnp.where(valid, coef, 0.0), (LANES, LANES)).T
    label = lax.broadcasted_iota(jnp.int32, (LANES, LANES), 0)
    for block in range(ids_ref.shape[0]):
        picked = jnp.where(label == ids_ref[block], coef, 0.0)
        grad_ref[block : block + 1, :] = jnp.sum(picked, axis=0, keepdims=True)


def swapped(pieces, axis):
    count = lax.axis_size(axis)
    out = [pieces[0]]
    for step in range(1, len(pieces)):
        route = [(i, i ^ step) for i in range(count)]
        out.append(lax.ppermute(pieces[step], axis, route))
    return out


def per_device(
    x_in,
    z_in,
    bc_in,
    dt_raw,
    dt_bias,
    a_log,
    conv_x,
    conv_bc,
    skip_gain,
    norm_gain,
    score_weight,
    passage_ids,
    teacher_logits,
    teacher_order,
):
    taps = conv_x.shape[0]
    count, width = x_in.shape
    heads = dt_raw.shape[1]
    groups = bc_in.shape[1]
    state_size = bc_in.shape[3]
    head_size = width // heads
    blocks = count // CH
    shards = lax.axis_size("seq")
    columns = lax.axis_size("head")
    half = shards // 2
    rows = state_size // half
    bc = bc_in.reshape(count, -1)
    bc_width = bc.shape[1]
    kbc = conv_bc.reshape(taps, -1)
    me = lax.axis_index("seq").astype(jnp.int32).reshape(1) % half
    ahead = [(i, i + 1) for i in range(shards - 1)]
    edge = jnp.concatenate([x_in[count - taps + 1 :], bc[count - taps + 1 :]], axis=1)
    halo = lax.ppermute(edge, "seq", ahead)

    smem = pl.BlockSpec(memory_space=pltpu.SMEM)

    def fixed(*shape):
        return pl.BlockSpec(shape, lambda i: (0,) * len(shape))

    def moving(*shape):
        return pl.BlockSpec(shape, lambda i: (i,) + (0,) * (len(shape) - 1))

    def shaped(dtype, *shape):
        return jax.ShapeDtypeStruct(shape, dtype)

    params = pltpu.CompilerParams(
        dimension_semantics=("arbitrary",), vmem_limit_bytes=VMEM_LIMIT
    )
    spread_scratch = pltpu.VMEM((LANES, width), BF16)
    outs = pl.pallas_call(
        partial(state_kernel, head_size=head_size, groups=groups),
        name="state",
        grid=(blocks,),
        in_specs=[
            smem,
            moving(CH, width),
            fixed(taps - 1, width + bc_width),
            moving(CH, bc_width),
            moving(CH, heads),
            fixed(1, heads),
            fixed(1, heads),
            fixed(taps, width),
            fixed(taps, bc_width),
        ],
        out_specs=[
            moving(CH, width),
            moving(CH, bc_width),
            moving(1, state_size, width),
            moving(CH, heads),
            moving(1, heads, CH),
            moving(CH, heads),
        ]
        + [fixed(rows, width + LANES)] * half,
        out_shape=[
            shaped(BF16, count, width),
            shaped(BF16, count, bc_width),
            shaped(BF16, blocks, state_size, width),
            shaped(F32, count, heads),
            shaped(F32, blocks, heads, CH),
            shaped(F32, count, heads),
        ]
        + [shaped(BF16, rows, width + LANES)] * half,
        scratch_shapes=[
            pltpu.VMEM((8, width), F32),
            pltpu.VMEM((8, bc_width), F32),
            pltpu.VMEM((state_size, width), F32),
            spread_scratch,
            pltpu.VMEM((8, LANES), F32),
        ],
        compiler_params=params,
        cost_estimate=pl.CostEstimate(flops=10**9, bytes_accessed=8 * 10**6, transcendentals=2 * 10**6),
    )(me, x_in, halo, bc, dt_raw, dt_bias[None], a_log[None], conv_x, kbc)
    xc, bcc, carry, cum, rowed, ecs = outs[:6]

    arrived = swapped(outs[6:], "seq")
    part, gain, low = pl.pallas_call(
        partial(prefix_kernel, head_size=head_size, heads=heads),
        name="prefix",
        in_specs=[smem] + [pl.BlockSpec(memory_space=pltpu.VMEM)] * half,
        out_specs=[pl.BlockSpec(memory_space=pltpu.VMEM)] * 3,
        out_shape=[
            shaped(F32, half, rows, width),
            shaped(F32, half, 1, width),
            shaped(BF16, rows, width),
        ],
        scratch_shapes=[
            pltpu.VMEM((half, rows, width), F32),
            pltpu.VMEM((half, rows, LANES), F32),
            spread_scratch,
        ],
        compiler_params=pltpu.CompilerParams(vmem_limit_bytes=VMEM_LIMIT),
        cost_estimate=pl.CostEstimate(flops=10**6, bytes_accessed=10**6, transcendentals=0),
    )(me, *arrived)
    low = lax.ppermute(low, "seq", [(i, i + half) for i in range(half)])
    back = pl.pallas_call(
        enter_kernel,
        name="enter",
        in_specs=[smem] + [pl.BlockSpec(memory_space=pltpu.VMEM)] * 3,
        out_specs=[pl.BlockSpec(memory_space=pltpu.VMEM)] * half,
        out_shape=[shaped(BF16, rows, width)] * half,
        compiler_params=pltpu.CompilerParams(vmem_limit_bytes=VMEM_LIMIT),
        cost_estimate=pl.CostEstimate(flops=10**6, bytes_accessed=10**6, transcendentals=0),
    )(me, part, gain, low)
    entering = swapped(back, "seq")

    y, p = pl.pallas_call(
        partial(inner_kernel, head_size=head_size, groups=groups),
        name="inner",
        grid=(blocks,),
        in_specs=[
            moving(CH, width),
            moving(CH, bc_width),
            moving(1, state_size, width),
            moving(CH, heads),
            moving(1, heads, CH),
            moving(CH, heads),
            moving(CH, width),
            fixed(1, heads),
        ],
        out_specs=[moving(CH, width), moving(CH, width)],
        out_shape=[shaped(F32, count, width), shaped(BF16, count, width)],
        scratch_shapes=[spread_scratch],
        compiler_params=params,
        cost_estimate=pl.CostEstimate(flops=5 * 10**9, bytes_accessed=20 * 10**6, transcendentals=4 * 10**6),
    )(xc, bcc, carry, cum, rowed, ecs, z_in, skip_gain[None])

    ids = passage_ids.reshape(blocks, 1, CH)
    mixed, sent = pl.pallas_call(
        partial(mix_kernel, groups=groups),
        name="mix",
        grid=(blocks,),
        in_specs=[
            smem,
            moving(CH, width),
            moving(CH, width),
            moving(CH, bc_width),
            fixed(1, width),
            fixed(1, width),
            moving(1, 1, CH),
        ]
        + [fixed(rows, width)] * half,
        out_specs=[moving(CH, width), fixed(shards * columns, 2, LANES)],
        out_shape=[
            shaped(BF16, count, width),
            shaped(F32, shards * columns, 2, LANES),
        ],
        scratch_shapes=[
            pltpu.VMEM((state_size, width), F32),
            pltpu.VMEM((state_size, width), BF16),
            pltpu.VMEM((CH, width), F32),
            pltpu.VMEM((2, LANES, LANES), F32),
        ],
        compiler_params=params,
        cost_estimate=pl.CostEstimate(flops=10**9, bytes_accessed=10 * 10**6, transcendentals=0),
    )(me, y, p, bcc, norm_gain[None], score_weight[None], ids, *entering)

    shared = lax.all_to_all(sent, ("seq", "head"), split_axis=0, concat_axis=0, tiled=True)
    grad, loss = pl.pallas_call(
        partial(loss_kernel, copies=columns, total=shards * count),
        name="loss",
        in_specs=[pl.BlockSpec(memory_space=pltpu.VMEM)] * 4,
        out_specs=[pl.BlockSpec(memory_space=pltpu.VMEM), smem],
        out_shape=[shaped(F32, blocks, LANES), shaped(F32, 1, 1)],
        compiler_params=pltpu.CompilerParams(vmem_limit_bytes=VMEM_LIMIT),
    )(shared, ids, teacher_logits[:, None], teacher_order[:, None])
    return (mixed, grad.reshape(count), loss.reshape(()))


def solution(mesh):
    placed = (
        P("seq", "head"),
        P("seq", "head"),
        P("seq", "head", None, None),
        P("seq", "head"),
        P("head"),
        P("head"),
        P(None, "head"),
        P(None, "head", None, None),
        P("head"),
        P("head"),
        P("head"),
        P("seq"),
        P(),
        P(),
    )
    return jax.shard_map(
        per_device,
        mesh=mesh,
        in_specs=placed,
        out_specs=(P("seq", "head"), P("seq"), P()),
        check_vma=False,
    )
```

```python
from functools import partial

import jax
import jax.numpy as jnp
from jax import lax
from jax.experimental import pallas as pl
from jax.experimental.pallas import tpu as pltpu
from jax.sharding import PartitionSpec as P

CH = 128
NP = 100
MIX_BLOCKS = 4
LANES = 128


EPS = 1e-05
CAP = 8.0

F32 = jnp.float32
BF16 = jnp.bfloat16
HIGH = lax.Precision.HIGHEST
VMEM_LIMIT = 24 * 1024 * 1024


def silu(v):
    half = 0.5 * v
    return half + half * jnp.tanh(half)


def dot(a, b, precision=None):
    return jnp.dot(a, b, preferred_element_type=F32, precision=precision)


def dot_rows(a, b):
    return lax.dot_general(a, b, (((1,), (1,)), ((), ())), preferred_element_type=F32)


def convolved(window, cur, taps):
    rows = cur.shape[0]
    cur = cur.astype(F32)
    window[8:, :] = cur
    half = taps[0:1] * window[5 : 5 + rows, :]
    half = half + taps[1:2] * window[6 : 6 + rows, :]
    half = half + taps[2:3] * window[7 : 7 + rows, :]
    half = half + taps[3:4] * cur
    return (half + half * jnp.tanh(half)).astype(BF16)


def packed(values, first, heads):
    values = pltpu.roll(values, LANES - first, 1)
    high = values.astype(BF16).astype(F32)
    low = pltpu.roll(values - high, heads, 1)
    lane = lax.broadcasted_iota(jnp.int32, values.shape, 1)
    return jnp.where(lane < heads, high, jnp.where(lane < 2 * heads, low, 0.0)).astype(BF16)


def fetches(source, target, sems):
    rows = [slice(start, start + CH) for start in range(0, target.shape[0], CH)]
    return [
        pltpu.make_async_copy(source.at[at, :], target.at[at, :], sems.at[k])
        for k, at in enumerate(rows)
    ]


def prep_kernel(
    x_hbm,
    dt_hbm,
    kx_hbm,
    kbc_hbm,
    bias_ref,
    alog_ref,
    skip_ref,
    x_ref,
    kx_ref,
    kbc_ref,
    spread_ref,
    cum_ref,
    row_ref,
    grown_ref,
    whole_ref,
    tails_ref,
    loads_ref,
    decay_ref,
    final_ref,
    skips_ref,
    dt,
    kx,
    kbc,
    sems,
    xsems,
    *,
    head_size,
):
    copies = [
        pltpu.make_async_copy(source, target, sems.at[k])
        for k, (source, target) in enumerate(
            ((dt_hbm, dt), (kx_hbm, kx), (kbc_hbm, kbc))
        )
    ]
    xs = fetches(x_hbm.at[:, : x_ref.shape[1]], x_ref, xsems)
    for copy in copies + xs:
        copy.start()
    heads, count = dt.shape
    blocks = count // CH
    used = blocks * heads
    shape = spread_ref.shape
    r = lax.broadcasted_iota(jnp.int32, shape, 0)
    c = lax.broadcasted_iota(jnp.int32, shape, 1)
    hit = (r % heads == c // head_size) & (r < 2 * heads)
    spread_ref[...] = jnp.where(hit, 1.0, 0.0).astype(BF16)
    gap = jnp.zeros((5, heads), F32)
    given = jnp.concatenate([bias_ref[...], alog_ref[...], skip_ref[...], gap], axis=0)
    given = jnp.concatenate([given, jnp.zeros((8, LANES - heads), F32)], axis=1)
    columns = given.T
    bias = jnp.concatenate([columns[:heads, 0:1]] * blocks, axis=0)
    scale = -jnp.exp(jnp.concatenate([columns[:heads, 1:2]] * blocks, axis=0))
    skips_ref[...] = dot(packed(given, 0, heads), spread_ref[...])[2:3]
    r = lax.broadcasted_iota(jnp.int32, (CH, CH), 0)
    c = lax.broadcasted_iota(jnp.int32, (CH, CH), 1)
    upper = jnp.where(r <= c, 1.0, 0.0)
    copies[0].wait()
    v = jnp.concatenate([dt[:, k * CH : (k + 1) * CH] for k in range(blocks)], axis=0) + bias
    steps = jnp.maximum(v, 0.0) + jnp.log1p(jnp.exp(-jnp.abs(v)))
    across = dot(scale * steps, upper, HIGH)
    row_ref[...] = across - jnp.log(steps)
    if used < LANES:
        pad = jnp.zeros((LANES - used, CH), F32)
        across = jnp.concatenate([across, pad], axis=0)
        steps = jnp.concatenate([steps, pad], axis=0)
    cum = across.T
    last = cum[CH - 1 :, :]
    before = jnp.zeros((1, LANES), F32)
    for k in range(1, blocks):
        before = before + jnp.where(
            lax.broadcasted_iota(jnp.int32, (1, LANES), 1) >= k * heads,
            pltpu.roll(last, k * heads, 1),
            0.0,
        )
    cum_ref[...] = cum
    steps = steps.T
    tails_ref[...] = jnp.exp(last - cum) * steps
    after = jnp.zeros((1, LANES), F32)
    for k in range(1, blocks):
        after = after + jnp.where(
            lax.broadcasted_iota(jnp.int32, (1, LANES), 1) < (blocks - k) * heads,
            pltpu.roll(last, LANES - k * heads, 1),
            0.0,
        )
    loads = jnp.exp(after + (last - cum)) * steps
    for k in range(blocks):
        loads_ref[k * CH : (k + 1) * CH, :] = packed(loads, k * heads, heads)
    grown_ref[...] = jnp.exp(cum)
    whole_ref[...] = jnp.exp(before + cum)
    decay = jnp.exp(jnp.broadcast_to(last, (8, LANES)))
    for k in range(blocks):
        decay_ref[8 * k : 8 * k + 8, :] = dot(packed(decay, k * heads, heads), spread_ref[...])
    final = jnp.exp(jnp.broadcast_to(before + last, (8, LANES)))
    final_ref[...] = packed(final, (blocks - 1) * heads, heads).astype(F32)
    copies[1].wait()
    kx_ref[...] = 0.5 * kx[...].astype(F32)
    copies[2].wait()
    for part in range(kbc_ref.shape[1] // LANES):
        at = slice(part * LANES, (part + 1) * LANES)
        kbc_ref[:, at] = 0.5 * kbc[:, part // 2, part % 2, :].astype(F32)
    for copy in xs:
        copy.wait()


def state_kernel(
    me_ref,
    x_ref,
    xhalo_ref,
    bc_ref,
    bchalo_ref,
    loads_ref,
    final_ref,
    kx_ref,
    kbc_ref,
    spread,
    *rest,
    following,
    passed,
):
    rest = rest[passed:]
    if following is not None:
        x_hbm, next_ref, sem = rest[0], rest[-5], rest[-1]
        rest = rest[1:-5] + rest[-4:-1]
        span = next_ref.shape[1]
        ahead = x_hbm.at[:, following * span : (following + 1) * span]
        copies = fetches(ahead, next_ref, sem)
        for copy in copies:
            copy.start()

    xc_ref, bmat_ref, *pieces, windows, trans, state = rest
    width = x_ref.shape[1]
    tiles = width // LANES
    halo = xhalo_ref.shape[0]
    windows[tiles, 8 - halo : 8, :] = bchalo_ref[...].astype(F32)
    done = convolved(windows.at[tiles], bc_ref[...], kbc_ref[...])
    bmat_ref[...] = done
    for start in range(0, done.shape[0], CH):
        part = done[start : start + CH].astype(F32).T
        trans[:, start : start + CH] = part.astype(BF16)
    rows = state.shape[0] // len(pieces)
    xhalo = xhalo_ref[...].astype(F32)
    for begin in range(0, width, 256):
        loads = []
        for start in (begin, begin + LANES):
            at = slice(start, start + LANES)
            window = windows.at[start // LANES]
            window[8 - halo : 8, :] = xhalo[:, at]
            done = convolved(window, x_ref[:, at], kx_ref[:, at])
            xc_ref[:, at] = done
            loads.append((done.astype(F32) * dot(loads_ref[...], spread[:, at])).astype(BF16))
        at = slice(begin, begin + 256)
        state[:, at] = dot(trans[...], jnp.concatenate(loads, axis=1))
    for k, piece in enumerate(pieces):
        owner = me_ref[0] ^ k
        take = state[pl.ds(pl.multiple_of(owner * rows, rows), rows), :]
        piece[:, :width] = take.astype(BF16)
        piece[:, width:] = jnp.broadcast_to(final_ref[0:1, :], (rows, LANES)).astype(BF16)
    if following is not None:
        for copy in copies:
            copy.wait()


def prefix_kernel(me_ref, spread, *rest, groups):
    size = len(rest) - 5
    pieces = rest[:size]
    part_ref, gain_ref, out_ref, states, decays = rest[size:]
    rows, width = out_ref.shape
    span = width // groups
    for step, piece in enumerate(pieces):
        owner = me_ref[0] ^ step
        for group in range(groups):
            start = group * (span + LANES)
            at = slice(group * span, (group + 1) * span)
            states[owner, :, at] = piece[:, start : start + span].astype(F32)
        decays[owner] = piece[:, span : span + LANES].astype(F32)
    held = jnp.zeros((rows, width), F32)
    gain = jnp.ones((1, width), F32)
    for shard in range(size):
        part_ref[shard] = held
        gain_ref[shard] = gain
        factor = dot(decays[shard].astype(BF16), spread[...])[0:1]
        held = factor * held + states[shard]
        gain = factor * gain
    out_ref[...] = held.astype(BF16)


def enter_kernel(me_ref, part_ref, gain_ref, low_ref, *outs):
    low = low_ref[...].astype(F32)
    for step, out in enumerate(outs):
        owner = me_ref[0] ^ step
        out[...] = (part_ref[owner] + gain_ref[owner] * low).astype(BF16)


def inner_kernel(
    xc_ref,
    bmat_ref,
    c_ref,
    chalo_ref,
    kc_ref,
    cum_ref,
    row_ref,
    grown_ref,
    whole_ref,
    tails_ref,
    decay_ref,
    z_ref,
    skips_ref,
    spread,
    y_ref,
    p_ref,
    cmat_ref,
    window,
    carry,
    *,
    head_size,
    first,
    heads,
):
    block = pl.program_id(0)
    width = xc_ref.shape[1]
    halo = chalo_ref.shape[0]

    @pl.when(block == 0)
    def _():
        window[8 - halo : 8, :] = chalo_ref[...].astype(F32)
        carry[...] = jnp.zeros_like(carry)

    cmat = convolved(window, c_ref[...], kc_ref[...])
    window[:8, :] = window[CH : CH + 8, :]
    cmat_ref[...] = cmat
    bmat = bmat_ref[...]
    trans = bmat.astype(F32).T.astype(BF16)
    cum = pltpu.roll(cum_ref[...], LANES - block * heads, 1)
    grown = packed(grown_ref[...], block * heads, heads)
    whole = packed(whole_ref[...], block * heads, heads)
    tails = packed(tails_ref[...], block * heads, heads)
    r = lax.broadcasted_iota(jnp.int32, (CH, CH), 0)
    c = lax.broadcasted_iota(jnp.int32, (CH, CH), 1)
    left = c < head_size
    per_tile = LANES // head_size
    pairs = jnp.where(r >= c, dot_rows(cmat, bmat), 0.0)
    for tile in range(width // LANES):
        at = slice(tile * LANES, (tile + 1) * LANES)
        xc = xc_ref[:, at]
        weights = []
        for head in range(first + tile * per_tile, first + (tile + 1) * per_tile):
            gap = cum[:, head : head + 1] - row_ref[head : head + 1, :]
            weights.append((pairs * jnp.exp(jnp.minimum(gap, 60.0))).astype(BF16))
        zero = jnp.zeros_like(xc)
        stacked = [jnp.where(left, xc, zero), jnp.where(left, zero, xc)]
        y = dot(jnp.concatenate(weights, axis=1), jnp.concatenate(stacked, axis=0))
        before = carry[:, at]
        y = y + dot(grown, spread[:, at]) * dot(cmat, before.astype(BF16))
        load = (xc.astype(F32) * dot(tails, spread[:, at])).astype(BF16)
        carry[:, at] = decay_ref[0:1, at] * before + dot(trans, load)
        y = y + skips_ref[:, at] * xc.astype(F32)
        gate = silu(z_ref[:, at].astype(F32))
        y_ref[:, at] = y * gate
        p_ref[:, at] = (gate * dot(whole, spread[:, at])).astype(BF16)


def mix_kernel(me_ref, y_ref, p_ref, cmat_ref, gain_ref, weight_ref, ids_ref, *rest, size, chained, final):
    pieces, rest = rest[:size], rest[size:]
    if chained:
        before_ref, rest = rest[0], rest[1:]
    mixed_ref, out_ref, wide, enter, gated, acc = rest
    block = pl.program_id(0)
    count, width = y_ref.shape
    rows = wide.shape[0] // size

    @pl.when(block == 0)
    def _():
        for step, piece in enumerate(pieces):
            owner = me_ref[0] ^ step
            wide[pl.ds(pl.multiple_of(owner * rows, rows), rows), :] = piece[...].astype(F32)
        enter[...] = wide[...].astype(BF16)
        acc[...] = before_ref[...] if chained else jnp.zeros_like(acc)

    cmat = cmat_ref[...]
    square = jnp.zeros((count, LANES), F32)
    for start in range(0, width, LANES):
        at = slice(start, start + LANES)
        g = y_ref[:, at] + p_ref[:, at].astype(F32) * dot(cmat, enter[:, at])
        gated[:, at] = g
        square = square + g * g
    scale = lax.rsqrt(jnp.sum(square, axis=1, keepdims=True) / width + EPS)
    scale = jnp.broadcast_to(scale, (count, LANES))
    read = jnp.zeros((count, LANES), F32)
    for start in range(0, width, LANES):
        at = slice(start, start + LANES)
        mixed = (gated[:, at] * scale * gain_ref[:, at].astype(F32)).astype(BF16)
        mixed_ref[:, at] = mixed
        read = read + mixed.astype(F32) * weight_ref[:, at].astype(F32)
    labels = lax.broadcasted_iota(jnp.int32, (LANES, count), 0)
    member = jnp.where(labels == ids_ref[0], 1.0, 0.0).astype(BF16)
    read = jnp.broadcast_to(jnp.sum(read, axis=1, keepdims=True), (count, LANES))
    high = read.astype(BF16).astype(F32)
    middle = (read - high).astype(BF16).astype(F32)
    lane = lax.broadcasted_iota(jnp.int32, (count, LANES), 1)
    terms = jnp.where(lane == 0, high, jnp.where(lane == 1, middle, read - high - middle))
    one = 1.0 if final else 0.0
    terms = jnp.where(lane == 3, one, jnp.where(lane > 3, 0.0, terms)).astype(BF16)
    acc[...] += dot(member, terms)

    @pl.when(block == pl.num_programs(0) - 1)
    def _():
        if final:
            flat = acc[...].T
            sums = flat[0:1] + flat[1:2] + flat[2:3]
            both = jnp.concatenate([sums, flat[3:4]], axis=0)
            out_ref[...] = jnp.broadcast_to(both[None], out_ref.shape)
        else:
            out_ref[...] = acc[...]


def flush_kernel(*refs):
    parts, out_ref, sems = refs[:-2], refs[-2], refs[-1]
    span = out_ref.shape[1] // len(parts)
    copies = [
        pltpu.make_async_copy(part, out_ref.at[:, k * span : (k + 1) * span], sems.at[k])
        for k, part in enumerate(parts)
    ]
    for copy in copies:
        copy.start()
    for copy in copies:
        copy.wait()


def loss_kernel(parts_ref, ids_ref, logits_ref, order_ref, grad_ref, loss_ref, *, copies, total):
    both = jnp.sum(parts_ref[...], axis=0)
    lane = lax.broadcasted_iota(jnp.int32, (1, LANES), 1)
    valid = lane < NP
    sums = both[0:1]
    counts = jnp.where(valid, both[1:2] / copies, 1.0)
    squash = jnp.tanh(sums / counts / CAP)
    scores = CAP * squash
    student = scores - jnp.log(jnp.sum(jnp.where(valid, jnp.exp(scores), 0.0)))
    hit = order_ref[...] == lax.broadcasted_iota(jnp.int32, (NP, LANES), 1)
    teacher = jnp.sum(jnp.where(hit, logits_ref[...], 0.0), axis=0, keepdims=True)
    teacher = teacher - jnp.log(jnp.sum(jnp.where(valid, jnp.exp(teacher), 0.0)))
    chance = jnp.where(valid, jnp.exp(teacher), 0.0)
    loss_ref[0, 0] = jnp.sum(chance * (teacher - student))
    coef = (jnp.exp(student) - chance) * (1.0 - squash * squash) * total / counts
    coef = jnp.broadcast_to(jnp.where(valid, coef, 0.0), (LANES, LANES)).T
    label = lax.broadcasted_iota(jnp.int32, (LANES, LANES), 0)
    for block in range(ids_ref.shape[0]):
        picked = jnp.where(label == ids_ref[block], coef, 0.0)
        grad_ref[block : block + 1, :] = jnp.sum(picked, axis=0, keepdims=True)


def swapped(pieces, axis):
    count = lax.axis_size(axis)
    out = [pieces[0]]
    for step in range(1, len(pieces)):
        route = [(i, i ^ step) for i in range(count)]
        out.append(lax.ppermute(pieces[step], axis, route))
    return out


def per_device(
    x_in,
    z_in,
    bc_in,
    dt_raw,
    dt_bias,
    a_log,
    conv_x,
    conv_bc,
    skip_gain,
    norm_gain,
    score_weight,
    passage_ids,
    teacher_logits,
    teacher_order,
):
    taps = conv_x.shape[0]
    count, width = x_in.shape
    groups = bc_in.shape[1]
    state_size = bc_in.shape[3]
    heads = dt_raw.shape[1] // groups
    span = width // groups
    head_size = span // heads
    pair = 2 * state_size
    blocks = count // CH
    shards = lax.axis_size("seq")
    columns = lax.axis_size("head")
    half = shards // 2
    rows = state_size // half
    bc = bc_in.reshape(count, -1)
    me = lax.axis_index("seq").astype(jnp.int32).reshape(1) % half
    ahead = [(i, i + 1) for i in range(shards - 1)]
    edge = jnp.concatenate([x_in[count - taps + 1 :], bc[count - taps + 1 :]], axis=1)
    halo = lax.ppermute(edge, "seq", ahead)
    ids = passage_ids.reshape(blocks, 1, CH)
    x_in, bc = lax.optimization_barrier((x_in, bc))

    smem = pl.BlockSpec(memory_space=pltpu.SMEM)
    vmem = pl.BlockSpec(memory_space=pltpu.VMEM)

    def block_of(shape, *index):
        return pl.BlockSpec(shape, lambda i: tuple(i if k is None else k for k in index))

    def hbm(array):
        return pltpu.with_memory_space_constraint(array, pltpu.HBM)

    def shaped(dtype, *shape):
        return jax.ShapeDtypeStruct(shape, dtype)

    def cost(flops, moved, steps=0):
        return pl.CostEstimate(flops=flops, bytes_accessed=moved, transcendentals=steps)

    params = pltpu.CompilerParams(
        dimension_semantics=("arbitrary",), vmem_limit_bytes=VMEM_LIMIT
    )
    plain = pltpu.CompilerParams(vmem_limit_bytes=VMEM_LIMIT)
    somewhere = pl.BlockSpec(memory_space=pl.ANY)
    every = groups * heads
    prepared = [
        shaped(BF16, count, span),
        shaped(F32, taps, width),
        shaped(F32, taps, groups * pair),
        shaped(BF16, LANES, width),
        shaped(F32, CH, LANES),
        shaped(F32, blocks * every, CH),
        shaped(F32, CH, LANES),
        shaped(F32, CH, LANES),
        shaped(F32, CH, LANES),
        shaped(BF16, count, LANES),
        shaped(F32, 8 * blocks, width),
        shaped(F32, 8, LANES),
        shaped(F32, 1, width),
    ]
    (x_here, kx, kbc, spread, cum, rowed, grown, whole, tails, loads, decay, final, skips) = pl.pallas_call(
        partial(prep_kernel, head_size=head_size),
        name="prep",
        grid=(1,),
        in_specs=[somewhere] * 4 + [block_of((1, every), 0, 0)] * 3,
        out_specs=[block_of(out.shape, *(0 for _ in out.shape)) for out in prepared],
        out_shape=prepared,
        scratch_shapes=[
            pltpu.VMEM((every, count), F32),
            pltpu.VMEM(conv_x.shape, BF16),
            pltpu.VMEM(conv_bc.shape, BF16),
            pltpu.SemaphoreType.DMA((3,)),
            pltpu.SemaphoreType.DMA((blocks,)),
        ],
        compiler_params=params,
        cost_estimate=cost(10**9, 4 * 10**6, 10**5),
    )(
        hbm(x_in),
        hbm(dt_raw.T),
        hbm(conv_x),
        hbm(conv_bc),
        hbm(dt_bias[None]),
        hbm(a_log[None]),
        hbm(skip_gain[None]),
    )

    def states(group, x_here, pieces):
        more = group + 1 < groups
        return pl.pallas_call(
            partial(
                state_kernel, following=group + 1 if more else None, passed=len(pieces)
            ),
            name="state%d" % group,
            grid=(1,),
            in_specs=[
                smem,
                block_of((count, span), 0, 0),
                block_of((taps - 1, span), 0, group),
                block_of((count, LANES), 0, 2 * group),
                block_of((taps - 1, LANES), 0, width // LANES + 2 * group),
                block_of((count, LANES), 0, 0),
                block_of((8, LANES), 0, 0),
                block_of((taps, span), 0, group),
                block_of((taps, LANES), 0, 2 * group),
                block_of((LANES, span), 0, group),
            ]
            + [somewhere] * len(pieces)
            + [somewhere] * more,
            out_specs=[block_of((count, span), 0, 0), block_of((count, LANES), 0, 0)]
            + [block_of((rows, span + LANES), 0, group)] * half
            + [block_of((count, span), 0, 0)] * more,
            out_shape=[shaped(BF16, count, span), shaped(BF16, count, LANES)]
            + [shaped(BF16, rows, groups * (span + LANES))] * half
            + [shaped(BF16, count, span)] * more,
            scratch_shapes=[
                pltpu.VMEM((span // LANES + 1, 8 + count, LANES), F32),
                pltpu.VMEM((state_size, count), BF16),
                pltpu.VMEM((state_size, span), F32),
            ]
            + [pltpu.SemaphoreType.DMA((blocks,))] * more,
            input_output_aliases={10 + k: 2 + k for k in range(len(pieces))},
            compiler_params=params,
            cost_estimate=cost(10**9, 4 * 10**6, 10**6),
        )(
            me,
            x_here,
            halo,
            bc,
            halo,
            loads,
            final,
            kx,
            kbc,
            spread,
            *pieces,
            *([hbm(x_in)] * more),
        )

    def prefix(arrived):
        return pl.pallas_call(
            partial(prefix_kernel, groups=groups),
            name="prefix",
            grid=(1,),
            in_specs=[smem, block_of((LANES, width), 0, 0)]
            + [block_of((rows, groups * (span + LANES)), 0, 0)] * half,
            out_specs=[
                block_of((half, rows, width), 0, 0, 0),
                block_of((half, 1, width), 0, 0, 0),
                block_of((rows, width), 0, 0),
            ],
            out_shape=[
                shaped(F32, half, rows, width),
                shaped(F32, half, 1, width),
                shaped(BF16, rows, width),
            ],
            scratch_shapes=[
                pltpu.VMEM((half, rows, width), F32),
                pltpu.VMEM((half, rows, LANES), F32),
            ],
            compiler_params=params,
            cost_estimate=cost(10**6, 10**6),
        )(me, spread, *arrived)

    def enter(part, gain, low):
        return pl.pallas_call(
            enter_kernel,
            name="enter",
            in_specs=[smem] + [vmem] * 3,
            out_specs=[vmem] * half,
            out_shape=[shaped(BF16, rows, width)] * half,
            compiler_params=plain,
            cost_estimate=cost(10**6, 10**6),
        )(me, part, gain, low)

    def inner(group, xc, bmat):
        return pl.pallas_call(
            partial(inner_kernel, head_size=head_size, first=group * heads, heads=every),
            name="inner%d" % group,
            grid=(blocks,),
            in_specs=[
                block_of((CH, span), None, 0),
                block_of((CH, LANES), None, 0),
                block_of((CH, LANES), None, 2 * group + 1),
                block_of((taps - 1, LANES), 0, width // LANES + 2 * group + 1),
                block_of((taps, LANES), 0, 2 * group + 1),
                block_of((CH, LANES), 0, 0),
                block_of((every, CH), None, 0),
                block_of((CH, LANES), 0, 0),
                block_of((CH, LANES), 0, 0),
                block_of((CH, LANES), 0, 0),
                block_of((8, span), None, group),
                block_of((CH, span), None, group),
                block_of((1, span), 0, group),
                block_of((LANES, span), 0, group),
            ],
            out_specs=[block_of((CH, span), None, 0)] * 2 + [block_of((CH, LANES), None, 0)],
            out_shape=[
                shaped(F32, count, span),
                shaped(BF16, count, span),
                shaped(BF16, count, LANES),
            ],
            scratch_shapes=[
                pltpu.VMEM((8 + CH, LANES), F32),
                pltpu.VMEM((state_size, span), F32),
            ],
            compiler_params=params,
            cost_estimate=cost(2 * 10**9, 10**7, 2 * 10**6),
        )(
            xc,
            bmat,
            bc,
            halo,
            kbc,
            cum,
            rowed,
            grown,
            whole,
            tails,
            decay,
            z_in,
            skips,
            spread,
        )

    mix_rows = MIX_BLOCKS * CH

    def mix(group, y, p, cmat, entering, before):
        final = group == groups - 1
        copies = shards * columns
        sent = (copies, 2, LANES) if final else (LANES, LANES)
        chained = before is not None
        extra = [block_of((LANES, LANES), 0, 0)]
        return pl.pallas_call(
            partial(mix_kernel, size=half, chained=chained, final=final),
            name="mix%d" % group,
            grid=(count // mix_rows,),
            in_specs=[
                smem,
                block_of((mix_rows, span), None, 0),
                block_of((mix_rows, span), None, 0),
                block_of((mix_rows, LANES), None, 0),
                block_of((1, span), 0, group),
                block_of((1, span), 0, group),
                block_of((1, 1, mix_rows), None, 0, 0),
            ]
            + [block_of((rows, span), 0, group)] * half
            + (extra if chained else []),
            out_specs=[block_of((mix_rows, span), None, 0), block_of(sent, *(0 for _ in sent))],
            out_shape=[shaped(BF16, count, span), shaped(F32, *sent)],
            scratch_shapes=[
                pltpu.VMEM((state_size, span), F32),
                pltpu.VMEM((state_size, span), BF16),
                pltpu.VMEM((mix_rows, span), F32),
                pltpu.VMEM((LANES, LANES), F32),
            ],
            compiler_params=params,
            cost_estimate=cost(5 * 10**8, 5 * 10**6),
        )(me, y, p, cmat, norm_gain[None], score_weight[None], passage_ids.reshape(-1, 1, mix_rows), *entering, *([before] if chained else []))

    lower = [(i, i + half) for i in range(half)]
    local, pieces = [], []
    for group in range(groups):
        local.append(states(group, x_here, pieces))
        pieces = local[-1][2 : 2 + half]
        x_here = local[-1][-1]
    within = [inner(group, *local[group][:2]) for group in range(groups)]
    arrived = swapped(pieces, "seq")
    *arrived, y = lax.optimization_barrier((*arrived, within[0][0]))
    within[0] = (y, *within[0][1:])
    part, gain, low = prefix(arrived)
    low = lax.ppermute(low, "seq", lower)
    if groups > 1:
        low, y = lax.optimization_barrier((low, within[1][0]))
        within[1] = (y, *within[1][1:])
    entering = swapped(enter(part, gain, low), "seq")
    sent, mixed = None, []
    for group in range(groups):
        done, sent = mix(group, *within[group], entering, sent)
        mixed.append(done)

    shared = lax.all_to_all(sent, ("seq", "head"), split_axis=0, concat_axis=0, tiled=True)
    mixed_out = pl.pallas_call(
        flush_kernel,
        name="flush",
        in_specs=[somewhere] * groups,
        out_specs=somewhere,
        out_shape=shaped(BF16, count, width),
        scratch_shapes=[pltpu.SemaphoreType.DMA((groups,))],
        compiler_params=plain,
        cost_estimate=cost(0, 4 * 10**6),
    )(*mixed)
    grad, loss = pl.pallas_call(
        partial(loss_kernel, copies=columns, total=shards * count),
        name="loss",
        in_specs=[vmem] * 4,
        out_specs=[vmem, smem],
        out_shape=[shaped(F32, blocks, LANES), shaped(F32, 1, 1)],
        compiler_params=plain,
    )(shared, ids, teacher_logits[:, None], teacher_order[:, None])
    return (mixed_out, grad.reshape(count), loss.reshape(()))


def solution(mesh):
    placed = (
        P("seq", "head"),
        P("seq", "head"),
        P("seq", "head", None, None),
        P("seq", "head"),
        P("head"),
        P("head"),
        P(None, "head"),
        P(None, "head", None, None),
        P("head"),
        P("head"),
        P("head"),
        P("seq"),
        P(),
        P(),
    )
    return jax.shard_map(
        per_device,
        mesh=mesh,
        in_specs=placed,
        out_specs=(P("seq", "head"), P("seq"), P()),
        check_vma=False,
    )
```

```python
from functools import partial

import jax
import jax.numpy as jnp
from jax import lax
from jax.experimental import pallas as pl
from jax.experimental.pallas import tpu as pltpu
from jax.sharding import PartitionSpec as P

CH = 128
NP = 100
MIX_BLOCKS = 4
LANES = 128


EPS = 1e-05
CAP = 8.0

F32 = jnp.float32
BF16 = jnp.bfloat16
HIGH = lax.Precision.HIGHEST
VMEM_LIMIT = 24 * 1024 * 1024


def silu(v):
    half = 0.5 * v
    return half + half * jnp.tanh(half)


def dot(a, b, precision=None):
    return jnp.dot(a, b, preferred_element_type=F32, precision=precision)


def dot_rows(a, b):
    return lax.dot_general(a, b, (((1,), (1,)), ((), ())), preferred_element_type=F32)


def convolved(window, cur, taps):
    rows = cur.shape[0]
    cur = cur.astype(F32)
    window[8:, :] = cur
    half = taps[0:1] * window[5 : 5 + rows, :]
    half = half + taps[1:2] * window[6 : 6 + rows, :]
    half = half + taps[2:3] * window[7 : 7 + rows, :]
    half = half + taps[3:4] * cur
    return (half + half * jnp.tanh(half)).astype(BF16)


def packed(values, first, heads):
    values = pltpu.roll(values, LANES - first, 1)
    high = values.astype(BF16).astype(F32)
    low = pltpu.roll(values - high, heads, 1)
    lane = lax.broadcasted_iota(jnp.int32, values.shape, 1)
    both = jnp.where(lane < heads, high, jnp.where(lane < 2 * heads, low, 0.0))
    return both[:, : 2 * heads].astype(BF16)


def prep_kernel(
    dt_hbm,
    kx_hbm,
    kbc_hbm,
    bias_hbm,
    alog_hbm,
    skip_hbm,
    kx_ref,
    kbc_ref,
    spread_ref,
    cum_ref,
    row_ref,
    grown_ref,
    whole_ref,
    tails_ref,
    loads_ref,
    decay_ref,
    final_ref,
    skips_ref,
    dt,
    kx,
    kbc,
    bias_row,
    alog_row,
    skip_row,
    sems,
    *,
    head_size,
):
    copies = [
        pltpu.make_async_copy(source, target, sems.at[k])
        for k, (source, target) in enumerate(
            (
                (dt_hbm, dt),
                (kx_hbm, kx),
                (kbc_hbm, kbc),
                (bias_hbm, bias_row),
                (alog_hbm, alog_row),
                (skip_hbm, skip_row),
            )
        )
    ]
    for copy in copies:
        copy.start()
    heads, count = dt.shape
    blocks = count // CH
    used = blocks * heads
    shape = spread_ref.shape
    r = lax.broadcasted_iota(jnp.int32, shape, 0)
    c = lax.broadcasted_iota(jnp.int32, shape, 1)
    hit = r % heads == c // head_size
    spread_ref[...] = jnp.where(hit, 1.0, 0.0).astype(BF16)
    for copy in copies[3:]:
        copy.wait()
    gap = jnp.zeros((5, heads), F32)
    given = jnp.concatenate([bias_row[...], alog_row[...], skip_row[...], gap], axis=0)
    given = jnp.concatenate([given, jnp.zeros((8, LANES - heads), F32)], axis=1)
    columns = given.T
    bias = jnp.concatenate([columns[:heads, 0:1]] * blocks, axis=0)
    scale = -jnp.exp(jnp.concatenate([columns[:heads, 1:2]] * blocks, axis=0))
    r = lax.broadcasted_iota(jnp.int32, (CH, CH), 0)
    c = lax.broadcasted_iota(jnp.int32, (CH, CH), 1)
    upper = jnp.where(r <= c, 1.0, 0.0).astype(BF16)
    copies[0].wait()
    v = jnp.concatenate([dt[:, k * CH : (k + 1) * CH] for k in range(blocks)], axis=0) + bias
    steps = jnp.maximum(v, 0.0) + jnp.log1p(jnp.exp(-jnp.abs(v)))
    rates = scale * steps
    high = rates.astype(BF16)
    left = rates - high.astype(F32)
    middle = left.astype(BF16)
    low = (left - middle.astype(F32)).astype(BF16)
    across = dot(jnp.concatenate([high, middle, low], axis=0), upper)
    across = (across[2 * used :] + across[used : 2 * used]) + across[:used]
    row_ref[...] = across - jnp.log(steps)
    if used < LANES:
        pad = jnp.zeros((LANES - used, CH), F32)
        across = jnp.concatenate([across, pad], axis=0)
        steps = jnp.concatenate([steps, pad], axis=0)
    cum = across.T
    last = cum[CH - 1 :, :]
    before = jnp.zeros((1, LANES), F32)
    for k in range(1, blocks):
        before = before + jnp.where(
            lax.broadcasted_iota(jnp.int32, (1, LANES), 1) >= k * heads,
            pltpu.roll(last, k * heads, 1),
            0.0,
        )
    cum_ref[...] = cum
    steps = steps.T
    tails_ref[...] = jnp.exp(last - cum) * steps
    after = jnp.zeros((1, LANES), F32)
    for k in range(1, blocks):
        after = after + jnp.where(
            lax.broadcasted_iota(jnp.int32, (1, LANES), 1) < (blocks - k) * heads,
            pltpu.roll(last, LANES - k * heads, 1),
            0.0,
        )
    loads = jnp.exp(after + (last - cum)) * steps
    for k in range(blocks):
        loads_ref[k * CH : (k + 1) * CH, :] = packed(loads, k * heads, heads)
    grown_ref[...] = jnp.exp(cum)
    whole_ref[...] = jnp.exp(before + cum)
    decay = jnp.exp(jnp.broadcast_to(last, (8, LANES)))
    rows = packed(jnp.broadcast_to(given[2:3], (8, LANES)), 0, heads)
    row = lax.broadcasted_iota(jnp.int32, rows.shape, 0)
    for k in range(blocks):
        mine = packed(decay, k * heads, heads).astype(F32)
        rows = jnp.where(row == k, mine, rows.astype(F32))
    rows = dot(rows.astype(BF16), spread_ref[...])
    for k in range(blocks):
        decay_ref[k] = rows[k : k + 1]
    skips_ref[...] = rows[blocks : blocks + 1]
    final = jnp.exp(jnp.broadcast_to(before + last, (8, LANES)))
    final = packed(final, (blocks - 1) * heads, heads).astype(F32)
    if 2 * heads < LANES:
        final = jnp.concatenate([final, jnp.zeros((8, LANES - 2 * heads), F32)], axis=1)
    final_ref[...] = final
    copies[1].wait()
    kx_ref[...] = 0.5 * kx[...].astype(F32)
    copies[2].wait()
    for part in range(kbc_ref.shape[1] // LANES):
        at = slice(part * LANES, (part + 1) * LANES)
        kbc_ref[:, at] = 0.5 * kbc[:, part // 2, part % 2, :].astype(F32)


def state_kernel(
    me_ref,
    x_ref,
    xhalo_ref,
    bc_ref,
    bchalo_ref,
    loads_ref,
    final_ref,
    kx_ref,
    kbc_ref,
    spread,
    *rest,
    passed,
):
    rest = rest[passed:]
    xc_ref, bmat_ref, *pieces, windows, trans, state = rest
    width = x_ref.shape[1]
    tiles = width // LANES
    halo = xhalo_ref.shape[0]
    windows[tiles, 8 - halo : 8, :] = bchalo_ref[...].astype(F32)
    done = convolved(windows.at[tiles], bc_ref[...], kbc_ref[...])
    bmat_ref[...] = done
    for start in range(0, done.shape[0], CH):
        part = done[start : start + CH].astype(F32).T
        trans[:, start : start + CH] = part.astype(BF16)
    rows = state.shape[0] // len(pieces)
    xhalo = xhalo_ref[...].astype(F32)
    for begin in range(0, width, 256):
        loads = []
        for start in (begin, begin + LANES):
            at = slice(start, start + LANES)
            window = windows.at[start // LANES]
            window[8 - halo : 8, :] = xhalo[:, at]
            done = convolved(window, x_ref[:, at], kx_ref[:, at])
            xc_ref[:, at] = done
            loads.append((done.astype(F32) * dot(loads_ref[...], spread[:, at])).astype(BF16))
        at = slice(begin, begin + 256)
        state[:, at] = dot(trans[...], jnp.concatenate(loads, axis=1))
    for k, piece in enumerate(pieces):
        owner = me_ref[0] ^ k
        take = state[pl.ds(pl.multiple_of(owner * rows, rows), rows), :]
        piece[:, :width] = take.astype(BF16)
        piece[:, width:] = jnp.broadcast_to(final_ref[0:1, :], (rows, LANES)).astype(BF16)


def prefix_kernel(me_ref, spread, *rest, groups):
    size = len(rest) - 5
    pieces = rest[:size]
    part_ref, gain_ref, out_ref, states, decays = rest[size:]
    rows, width = out_ref.shape
    span = width // groups
    for step, piece in enumerate(pieces):
        owner = me_ref[0] ^ step
        for group in range(groups):
            start = group * (span + LANES)
            at = slice(group * span, (group + 1) * span)
            states[owner, :, at] = piece[:, start : start + span].astype(F32)
        decays[owner] = piece[:, span : span + LANES].astype(F32)
    held = jnp.zeros((rows, width), F32)
    gain = jnp.ones((1, width), F32)
    for shard in range(size):
        part_ref[shard] = held
        gain_ref[shard] = gain
        factor = dot(decays[shard, :, : spread.shape[0]].astype(BF16), spread[...])[0:1]
        held = factor * held + states[shard]
        gain = factor * gain
    out_ref[...] = held.astype(BF16)


def enter_kernel(me_ref, part_ref, gain_ref, low_ref, *outs):
    low = low_ref[...].astype(F32)
    for step, out in enumerate(outs):
        owner = me_ref[0] ^ step
        out[...] = (part_ref[owner] + gain_ref[owner] * low).astype(BF16)


def inner_kernel(
    xc_ref,
    bmat_ref,
    c_ref,
    chalo_ref,
    kc_ref,
    cum_ref,
    row_ref,
    grown_ref,
    whole_ref,
    tails_ref,
    decay_ref,
    z_ref,
    skips_ref,
    spread,
    y_ref,
    p_ref,
    cmat_ref,
    window,
    carry,
    *,
    head_size,
    first,
    heads,
):
    block = pl.program_id(0)
    width = xc_ref.shape[1]
    halo = chalo_ref.shape[0]

    @pl.when(block == 0)
    def _():
        window[8 - halo : 8, :] = chalo_ref[...].astype(F32)
        carry[...] = jnp.zeros_like(carry)

    cmat = convolved(window, c_ref[...], kc_ref[...])
    window[:8, :] = window[CH : CH + 8, :]
    cmat_ref[...] = cmat
    bmat = bmat_ref[...]
    trans = bmat.astype(F32).T.astype(BF16)
    cum = pltpu.roll(cum_ref[...], LANES - block * heads, 1)
    grown = packed(grown_ref[...], block * heads, heads)
    whole = packed(whole_ref[...], block * heads, heads)
    tails = packed(tails_ref[...], block * heads, heads)
    r = lax.broadcasted_iota(jnp.int32, (CH, CH), 0)
    c = lax.broadcasted_iota(jnp.int32, (CH, CH), 1)
    left = c < head_size
    per_tile = LANES // head_size
    pairs = jnp.where(r >= c, dot_rows(cmat, bmat), 0.0)
    for tile in range(width // LANES):
        at = slice(tile * LANES, (tile + 1) * LANES)
        xc = xc_ref[:, at]
        weights = []
        for head in range(first + tile * per_tile, first + (tile + 1) * per_tile):
            gap = cum[:, head : head + 1] - row_ref[head : head + 1, :]
            weights.append((pairs * jnp.exp(jnp.minimum(gap, 60.0))).astype(BF16))
        zero = jnp.zeros_like(xc)
        stacked = [jnp.where(left, xc, zero), jnp.where(left, zero, xc)]
        y = dot(jnp.concatenate(weights, axis=1), jnp.concatenate(stacked, axis=0))
        before = carry[:, at]
        y = y + dot(grown, spread[:, at]) * dot(cmat, before.astype(BF16))
        load = (xc.astype(F32) * dot(tails, spread[:, at])).astype(BF16)
        carry[:, at] = decay_ref[0, :, at] * before + dot(trans, load)
        y = y + skips_ref[:, at] * xc.astype(F32)
        gate = silu(z_ref[:, at].astype(F32))
        y_ref[:, at] = y * gate
        p_ref[:, at] = (gate * dot(whole, spread[:, at])).astype(BF16)


def mix_kernel(me_ref, y_ref, p_ref, cmat_ref, gain_ref, weight_ref, ids_ref, *rest, size, chained, final):
    pieces, rest = rest[:size], rest[size:]
    if chained:
        before_ref, rest = rest[0], rest[1:]
    mixed_ref, out_ref, wide, enter, gated, acc = rest
    block = pl.program_id(0)
    count, width = y_ref.shape
    rows = wide.shape[0] // size

    @pl.when(block == 0)
    def _():
        for step, piece in enumerate(pieces):
            owner = me_ref[0] ^ step
            wide[pl.ds(pl.multiple_of(owner * rows, rows), rows), :] = piece[...].astype(F32)
        enter[...] = wide[...].astype(BF16)
        acc[...] = before_ref[...] if chained else jnp.zeros_like(acc)

    cmat = cmat_ref[...]
    square = jnp.zeros((count, LANES), F32)
    for start in range(0, width, LANES):
        at = slice(start, start + LANES)
        g = y_ref[:, at] + p_ref[:, at].astype(F32) * dot(cmat, enter[:, at])
        gated[:, at] = g
        square = square + g * g
    scale = lax.rsqrt(jnp.sum(square, axis=1, keepdims=True) / width + EPS)
    scale = jnp.broadcast_to(scale, (count, LANES))
    read = jnp.zeros((count, LANES), F32)
    for start in range(0, width, LANES):
        at = slice(start, start + LANES)
        mixed = (gated[:, at] * scale * gain_ref[:, at].astype(F32)).astype(BF16)
        mixed_ref[:, at] = mixed
        read = read + mixed.astype(F32) * weight_ref[:, at].astype(F32)
    labels = lax.broadcasted_iota(jnp.int32, (LANES, count), 0)
    member = jnp.where(labels == ids_ref[0], 1.0, 0.0).astype(BF16)
    read = jnp.broadcast_to(jnp.sum(read, axis=1, keepdims=True), (count, LANES))
    high = read.astype(BF16).astype(F32)
    middle = (read - high).astype(BF16).astype(F32)
    lane = lax.broadcasted_iota(jnp.int32, (count, LANES), 1)
    terms = jnp.where(lane == 0, high, jnp.where(lane == 1, middle, read - high - middle))
    one = 1.0 if final else 0.0
    terms = jnp.where(lane == 3, one, jnp.where(lane > 3, 0.0, terms)).astype(BF16)
    acc[...] += dot(member, terms)

    @pl.when(block == pl.num_programs(0) - 1)
    def _():
        if final:
            flat = acc[...].T
            sums = flat[0:1] + flat[1:2] + flat[2:3]
            both = jnp.concatenate([sums, flat[3:4]], axis=0)
            out_ref[...] = jnp.broadcast_to(both[None], out_ref.shape)
        else:
            out_ref[...] = acc[...]


def flush_kernel(*refs):
    parts, out_ref, sems = refs[:-2], refs[-2], refs[-1]
    span = out_ref.shape[1] // len(parts)
    copies = [
        pltpu.make_async_copy(part, out_ref.at[:, k * span : (k + 1) * span], sems.at[k])
        for k, part in enumerate(parts)
    ]
    for copy in copies:
        copy.start()
    for copy in copies:
        copy.wait()


def loss_kernel(parts_ref, ids_ref, logits_ref, order_ref, grad_ref, loss_ref, *, copies, total):
    both = jnp.sum(parts_ref[...], axis=0)
    lane = lax.broadcasted_iota(jnp.int32, (1, LANES), 1)
    valid = lane < NP
    sums = both[0:1]
    counts = jnp.where(valid, both[1:2] / copies, 1.0)
    squash = jnp.tanh(sums / counts / CAP)
    scores = CAP * squash
    student = scores - jnp.log(jnp.sum(jnp.where(valid, jnp.exp(scores), 0.0)))
    hit = order_ref[...] == lax.broadcasted_iota(jnp.int32, (NP, LANES), 1)
    teacher = jnp.sum(jnp.where(hit, logits_ref[...], 0.0), axis=0, keepdims=True)
    teacher = teacher - jnp.log(jnp.sum(jnp.where(valid, jnp.exp(teacher), 0.0)))
    chance = jnp.where(valid, jnp.exp(teacher), 0.0)
    loss_ref[0, 0] = jnp.sum(chance * (teacher - student))
    coef = (jnp.exp(student) - chance) * (1.0 - squash * squash) * total / counts
    coef = jnp.broadcast_to(jnp.where(valid, coef, 0.0), (LANES, LANES)).T
    label = lax.broadcasted_iota(jnp.int32, (LANES, LANES), 0)
    for block in range(ids_ref.shape[0]):
        picked = jnp.where(label == ids_ref[block], coef, 0.0)
        grad_ref[block : block + 1, :] = jnp.sum(picked, axis=0, keepdims=True)


def swapped(pieces, axis):
    count = lax.axis_size(axis)
    out = [pieces[0]]
    for step in range(1, len(pieces)):
        route = [(i, i ^ step) for i in range(count)]
        out.append(lax.ppermute(pieces[step], axis, route))
    return out


def per_device(
    x_in,
    z_in,
    bc_in,
    dt_raw,
    dt_bias,
    a_log,
    conv_x,
    conv_bc,
    skip_gain,
    norm_gain,
    score_weight,
    passage_ids,
    teacher_logits,
    teacher_order,
):
    taps = conv_x.shape[0]
    count, width = x_in.shape
    groups = bc_in.shape[1]
    state_size = bc_in.shape[3]
    heads = dt_raw.shape[1] // groups
    span = width // groups
    head_size = span // heads
    pair = 2 * state_size
    blocks = count // CH
    shards = lax.axis_size("seq")
    columns = lax.axis_size("head")
    half = shards // 2
    rows = state_size // half
    bc = bc_in.reshape(count, -1)
    me = lax.axis_index("seq").astype(jnp.int32).reshape(1) % half
    ahead = [(i, i + 1) for i in range(shards - 1)]
    edge = jnp.concatenate([x_in[count - taps + 1 :], bc[count - taps + 1 :]], axis=1)
    halo = lax.ppermute(edge, "seq", ahead)
    ids = passage_ids.reshape(blocks, 1, CH)
    x_in, bc = lax.optimization_barrier((x_in, bc))

    smem = pl.BlockSpec(memory_space=pltpu.SMEM)
    vmem = pl.BlockSpec(memory_space=pltpu.VMEM)

    def block_of(shape, *index):
        return pl.BlockSpec(shape, lambda i: tuple(i if k is None else k for k in index))

    def hbm(array):
        return pltpu.with_memory_space_constraint(array, pltpu.HBM)

    def shaped(dtype, *shape):
        return jax.ShapeDtypeStruct(shape, dtype)

    def cost(flops, moved, steps=0):
        return pl.CostEstimate(flops=flops, bytes_accessed=moved, transcendentals=steps)

    params = pltpu.CompilerParams(
        dimension_semantics=("arbitrary",), vmem_limit_bytes=VMEM_LIMIT
    )
    plain = pltpu.CompilerParams(vmem_limit_bytes=VMEM_LIMIT)
    somewhere = pl.BlockSpec(memory_space=pl.ANY)
    every = groups * heads
    prepared = [
        shaped(F32, taps, width),
        shaped(F32, taps, groups * pair),
        shaped(BF16, 2 * every, width),
        shaped(F32, CH, LANES),
        shaped(F32, blocks * every, CH),
        shaped(F32, CH, LANES),
        shaped(F32, CH, LANES),
        shaped(F32, CH, LANES),
        shaped(BF16, count, 2 * every),
        shaped(F32, blocks, 1, width),
        shaped(F32, 8, LANES),
        shaped(F32, 1, width),
    ]
    (kx, kbc, spread, cum, rowed, grown, whole, tails, loads, decay, final, skips) = pl.pallas_call(
        partial(prep_kernel, head_size=head_size),
        name="prep",
        grid=(1,),
        in_specs=[somewhere] * 6,
        out_specs=[block_of(out.shape, *(0 for _ in out.shape)) for out in prepared],
        out_shape=prepared,
        scratch_shapes=[
            pltpu.VMEM((every, count), F32),
            pltpu.VMEM(conv_x.shape, BF16),
            pltpu.VMEM(conv_bc.shape, BF16),
            pltpu.VMEM((1, every), F32),
            pltpu.VMEM((1, every), F32),
            pltpu.VMEM((1, every), F32),
            pltpu.SemaphoreType.DMA((6,)),
        ],
        compiler_params=params,
        cost_estimate=cost(10**9, 4 * 10**6, 10**5),
    )(
        hbm(dt_raw.T),
        hbm(conv_x),
        hbm(conv_bc),
        hbm(dt_bias[None]),
        hbm(a_log[None]),
        hbm(skip_gain[None]),
    )

    def states(group, pieces):
        return pl.pallas_call(
            partial(state_kernel, passed=len(pieces)),
            name="state%d" % group,
            grid=(1,),
            in_specs=[
                smem,
                block_of((count, span), 0, group),
                block_of((taps - 1, span), 0, group),
                block_of((count, LANES), 0, 2 * group),
                block_of((taps - 1, LANES), 0, width // LANES + 2 * group),
                block_of((count, 2 * every), 0, 0),
                block_of((8, LANES), 0, 0),
                block_of((taps, span), 0, group),
                block_of((taps, LANES), 0, 2 * group),
                block_of((2 * every, span), 0, group),
            ]
            + [somewhere] * len(pieces),
            out_specs=[block_of((count, span), 0, 0), block_of((count, LANES), 0, 0)]
            + [block_of((rows, span + LANES), 0, group)] * half,
            out_shape=[shaped(BF16, count, span), shaped(BF16, count, LANES)]
            + [shaped(BF16, rows, groups * (span + LANES))] * half,
            scratch_shapes=[
                pltpu.VMEM((span // LANES + 1, 8 + count, LANES), F32),
                pltpu.VMEM((state_size, count), BF16),
                pltpu.VMEM((state_size, span), F32),
            ],
            input_output_aliases={10 + k: 2 + k for k in range(len(pieces))},
            compiler_params=params,
            cost_estimate=cost(10**9, 4 * 10**6, 10**6),
        )(
            me,
            x_in,
            halo,
            bc,
            halo,
            loads,
            final,
            kx,
            kbc,
            spread,
            *pieces,
        )

    def prefix(arrived):
        return pl.pallas_call(
            partial(prefix_kernel, groups=groups),
            name="prefix",
            grid=(1,),
            in_specs=[smem, block_of((2 * every, width), 0, 0)]
            + [block_of((rows, groups * (span + LANES)), 0, 0)] * half,
            out_specs=[
                block_of((half, rows, width), 0, 0, 0),
                block_of((half, 1, width), 0, 0, 0),
                block_of((rows, width), 0, 0),
            ],
            out_shape=[
                shaped(F32, half, rows, width),
                shaped(F32, half, 1, width),
                shaped(BF16, rows, width),
            ],
            scratch_shapes=[
                pltpu.VMEM((half, rows, width), F32),
                pltpu.VMEM((half, rows, LANES), F32),
            ],
            compiler_params=params,
            cost_estimate=cost(10**6, 10**6),
        )(me, spread, *arrived)

    def enter(part, gain, low):
        return pl.pallas_call(
            enter_kernel,
            name="enter",
            in_specs=[smem] + [vmem] * 3,
            out_specs=[vmem] * half,
            out_shape=[shaped(BF16, rows, width)] * half,
            compiler_params=plain,
            cost_estimate=cost(10**6, 10**6),
        )(me, part, gain, low)

    def inner(group, xc, bmat):
        return pl.pallas_call(
            partial(inner_kernel, head_size=head_size, first=group * heads, heads=every),
            name="inner%d" % group,
            grid=(blocks,),
            in_specs=[
                block_of((CH, span), None, 0),
                block_of((CH, LANES), None, 0),
                block_of((CH, LANES), None, 2 * group + 1),
                block_of((taps - 1, LANES), 0, width // LANES + 2 * group + 1),
                block_of((taps, LANES), 0, 2 * group + 1),
                block_of((CH, LANES), 0, 0),
                block_of((every, CH), None, 0),
                block_of((CH, LANES), 0, 0),
                block_of((CH, LANES), 0, 0),
                block_of((CH, LANES), 0, 0),
                block_of((1, 1, span), None, 0, group),
                block_of((CH, span), None, group),
                block_of((1, span), 0, group),
                block_of((2 * every, span), 0, group),
            ],
            out_specs=[block_of((CH, span), None, 0)] * 2 + [block_of((CH, LANES), None, 0)],
            out_shape=[
                shaped(F32, count, span),
                shaped(BF16, count, span),
                shaped(BF16, count, LANES),
            ],
            scratch_shapes=[
                pltpu.VMEM((8 + CH, LANES), F32),
                pltpu.VMEM((state_size, span), F32),
            ],
            compiler_params=params,
            cost_estimate=cost(2 * 10**9, 10**7, 2 * 10**6),
        )(
            xc,
            bmat,
            bc,
            halo,
            kbc,
            cum,
            rowed,
            grown,
            whole,
            tails,
            decay,
            z_in,
            skips,
            spread,
        )

    mix_rows = MIX_BLOCKS * CH

    def mix(group, y, p, cmat, entering, before):
        final = group == groups - 1
        copies = shards * columns
        sent = (copies, 2, LANES) if final else (LANES, LANES)
        chained = before is not None
        extra = [block_of((LANES, LANES), 0, 0)]
        return pl.pallas_call(
            partial(mix_kernel, size=half, chained=chained, final=final),
            name="mix%d" % group,
            grid=(count // mix_rows,),
            in_specs=[
                smem,
                block_of((mix_rows, span), None, 0),
                block_of((mix_rows, span), None, 0),
                block_of((mix_rows, LANES), None, 0),
                block_of((1, span), 0, group),
                block_of((1, span), 0, group),
                block_of((1, 1, mix_rows), None, 0, 0),
            ]
            + [block_of((rows, span), 0, group)] * half
            + (extra if chained else []),
            out_specs=[block_of((mix_rows, span), None, 0), block_of(sent, *(0 for _ in sent))],
            out_shape=[shaped(BF16, count, span), shaped(F32, *sent)],
            scratch_shapes=[
                pltpu.VMEM((state_size, span), F32),
                pltpu.VMEM((state_size, span), BF16),
                pltpu.VMEM((mix_rows, span), F32),
                pltpu.VMEM((LANES, LANES), F32),
            ],
            compiler_params=params,
            cost_estimate=cost(5 * 10**8, 5 * 10**6),
        )(me, y, p, cmat, norm_gain[None], score_weight[None], passage_ids.reshape(-1, 1, mix_rows), *entering, *([before] if chained else []))

    lower = [(i, i + half) for i in range(half)]
    local, pieces = [], []
    for group in range(groups):
        local.append(states(group, pieces))
        pieces = local[-1][2:]
    within = [inner(group, *local[group][:2]) for group in range(groups)]
    arrived = swapped(pieces, "seq")
    *arrived, y = lax.optimization_barrier((*arrived, within[0][0]))
    within[0] = (y, *within[0][1:])
    part, gain, low = prefix(arrived)
    low = lax.ppermute(low, "seq", lower)
    if groups > 1:
        low, y = lax.optimization_barrier((low, within[1][0]))
        within[1] = (y, *within[1][1:])
    entering = swapped(enter(part, gain, low), "seq")
    sent, mixed = None, []
    for group in range(groups):
        done, sent = mix(group, *within[group], entering, sent)
        mixed.append(done)

    shared = lax.all_to_all(sent, ("seq", "head"), split_axis=0, concat_axis=0, tiled=True)
    mixed_out = pl.pallas_call(
        flush_kernel,
        name="flush",
        in_specs=[somewhere] * groups,
        out_specs=somewhere,
        out_shape=shaped(BF16, count, width),
        scratch_shapes=[pltpu.SemaphoreType.DMA((groups,))],
        compiler_params=plain,
        cost_estimate=cost(0, 4 * 10**6),
    )(*mixed)
    grad, loss = pl.pallas_call(
        partial(loss_kernel, copies=columns, total=shards * count),
        name="loss",
        in_specs=[vmem] * 4,
        out_specs=[vmem, smem],
        out_shape=[shaped(F32, blocks, LANES), shaped(F32, 1, 1)],
        compiler_params=plain,
    )(shared, ids, teacher_logits[:, None], teacher_order[:, None])
    return (mixed_out, grad.reshape(count), loss.reshape(()))


def solution(mesh):
    placed = (
        P("seq", "head"),
        P("seq", "head"),
        P("seq", "head", None, None),
        P("seq", "head"),
        P("head"),
        P("head"),
        P(None, "head"),
        P(None, "head", None, None),
        P("head"),
        P("head"),
        P("head"),
        P("seq"),
        P(),
        P(),
    )
    return jax.shard_map(
        per_device,
        mesh=mesh,
        in_specs=placed,
        out_specs=(P("seq", "head"), P("seq"), P()),
        check_vma=False,
    )
```

```python
from functools import partial

import jax
import jax.numpy as jnp
from jax import lax
from jax.experimental import pallas as pl
from jax.experimental.pallas import tpu as pltpu
from jax.sharding import PartitionSpec as P

CH = 128
NP = 100
MIX_BLOCKS = 4
LANES = 128


EPS = 1e-05
CAP = 8.0

F32 = jnp.float32
BF16 = jnp.bfloat16
HIGH = lax.Precision.HIGHEST
VMEM_LIMIT = 24 * 1024 * 1024


def silu(v):
    half = 0.5 * v
    return half + half * jnp.tanh(half)


def dot(a, b, precision=None):
    return jnp.dot(a, b, preferred_element_type=F32, precision=precision)


def dot_rows(a, b):
    return lax.dot_general(a, b, (((1,), (1,)), ((), ())), preferred_element_type=F32)


def convolved(window, cur, taps):
    rows = cur.shape[0]
    cur = cur.astype(F32)
    window[8:, :] = cur
    half = taps[0:1] * window[5 : 5 + rows, :]
    half = half + taps[1:2] * window[6 : 6 + rows, :]
    half = half + taps[2:3] * window[7 : 7 + rows, :]
    half = half + taps[3:4] * cur
    return (half + half * jnp.tanh(half)).astype(BF16)


def packed(values, first, heads):
    values = pltpu.roll(values, LANES - first, 1)
    high = values.astype(BF16).astype(F32)
    low = pltpu.roll(values - high, heads, 1)
    lane = lax.broadcasted_iota(jnp.int32, values.shape, 1)
    both = jnp.where(lane < heads, high, jnp.where(lane < 2 * heads, low, 0.0))
    return both[:, : 2 * heads].astype(BF16)


def prep_kernel(
    dt_hbm,
    kx_hbm,
    kbc_hbm,
    bias_hbm,
    alog_hbm,
    skip_hbm,
    kx_ref,
    kbc_ref,
    spread_ref,
    cum_ref,
    row_ref,
    grown_ref,
    whole_ref,
    tails_ref,
    loads_ref,
    decay_ref,
    final_ref,
    skips_ref,
    dt,
    kx,
    kbc,
    bias_row,
    alog_row,
    skip_row,
    sems,
    *,
    head_size,
):
    copies = [
        pltpu.make_async_copy(source, target, sems.at[k])
        for k, (source, target) in enumerate(
            (
                (dt_hbm, dt),
                (kx_hbm, kx),
                (kbc_hbm, kbc),
                (bias_hbm, bias_row),
                (alog_hbm, alog_row),
                (skip_hbm, skip_row),
            )
        )
    ]
    for copy in copies:
        copy.start()
    heads, count = dt.shape
    blocks = count // CH
    used = blocks * heads
    shape = spread_ref.shape
    r = lax.broadcasted_iota(jnp.int32, shape, 0)
    c = lax.broadcasted_iota(jnp.int32, shape, 1)
    hit = r % heads == c // head_size
    spread_ref[...] = jnp.where(hit, 1.0, 0.0).astype(BF16)
    for copy in copies[3:]:
        copy.wait()
    gap = jnp.zeros((5, heads), F32)
    given = jnp.concatenate([bias_row[...], alog_row[...], skip_row[...], gap], axis=0)
    given = jnp.concatenate([given, jnp.zeros((8, LANES - heads), F32)], axis=1)
    columns = given.T
    bias = jnp.concatenate([columns[:heads, 0:1]] * blocks, axis=0)
    scale = -jnp.exp(jnp.concatenate([columns[:heads, 1:2]] * blocks, axis=0))
    r = lax.broadcasted_iota(jnp.int32, (CH, CH), 0)
    c = lax.broadcasted_iota(jnp.int32, (CH, CH), 1)
    upper = jnp.where(r <= c, 1.0, 0.0).astype(BF16)
    copies[0].wait()
    v = jnp.concatenate([dt[:, k * CH : (k + 1) * CH] for k in range(blocks)], axis=0) + bias
    steps = jnp.maximum(v, 0.0) + jnp.log1p(jnp.exp(-jnp.abs(v)))
    rates = scale * steps
    high = rates.astype(BF16)
    left = rates - high.astype(F32)
    middle = left.astype(BF16)
    low = (left - middle.astype(F32)).astype(BF16)
    across = dot(jnp.concatenate([high, middle, low], axis=0), upper)
    across = (across[2 * used :] + across[used : 2 * used]) + across[:used]
    row_ref[...] = across - jnp.log(steps)
    if used < LANES:
        pad = jnp.zeros((LANES - used, CH), F32)
        across = jnp.concatenate([across, pad], axis=0)
        steps = jnp.concatenate([steps, pad], axis=0)
    cum = across.T
    last = cum[CH - 1 :, :]
    before = jnp.zeros((1, LANES), F32)
    for k in range(1, blocks):
        before = before + jnp.where(
            lax.broadcasted_iota(jnp.int32, (1, LANES), 1) >= k * heads,
            pltpu.roll(last, k * heads, 1),
            0.0,
        )
    cum_ref[...] = cum
    steps = steps.T
    tails_ref[...] = jnp.exp(last - cum) * steps
    after = jnp.zeros((1, LANES), F32)
    for k in range(1, blocks):
        after = after + jnp.where(
            lax.broadcasted_iota(jnp.int32, (1, LANES), 1) < (blocks - k) * heads,
            pltpu.roll(last, LANES - k * heads, 1),
            0.0,
        )
    loads = jnp.exp(after + (last - cum)) * steps
    for k in range(blocks):
        loads_ref[k * CH : (k + 1) * CH, :] = packed(loads, k * heads, heads)
    grown_ref[...] = jnp.exp(cum)
    whole_ref[...] = jnp.exp(before + cum)
    decay = jnp.exp(jnp.broadcast_to(last, (8, LANES)))
    rows = packed(jnp.broadcast_to(given[2:3], (8, LANES)), 0, heads)
    row = lax.broadcasted_iota(jnp.int32, rows.shape, 0)
    for k in range(blocks):
        mine = packed(decay, k * heads, heads).astype(F32)
        rows = jnp.where(row == k, mine, rows.astype(F32))
    rows = dot(rows.astype(BF16), spread_ref[...])
    for k in range(blocks):
        decay_ref[k] = rows[k : k + 1]
    skips_ref[...] = rows[blocks : blocks + 1]
    final = jnp.exp(jnp.broadcast_to(before + last, (8, LANES)))
    final = packed(final, (blocks - 1) * heads, heads).astype(F32)
    if 2 * heads < LANES:
        final = jnp.concatenate([final, jnp.zeros((8, LANES - 2 * heads), F32)], axis=1)
    final_ref[...] = final
    copies[1].wait()
    kx_ref[...] = 0.5 * kx[...].astype(F32)
    copies[2].wait()
    for part in range(kbc_ref.shape[1] // LANES):
        at = slice(part * LANES, (part + 1) * LANES)
        kbc_ref[:, at] = 0.5 * kbc[:, part // 2, part % 2, :].astype(F32)


def state_kernel(
    me_ref,
    x_ref,
    xhalo_ref,
    bc_ref,
    bchalo_ref,
    loads_ref,
    final_ref,
    kx_ref,
    kbc_ref,
    spread,
    *rest,
    passed,
):
    rest = rest[passed:]
    xc_ref, bmat_ref, *pieces, windows, trans, state = rest
    width = x_ref.shape[1]
    tiles = width // LANES
    halo = xhalo_ref.shape[0]
    windows[tiles, 8 - halo : 8, :] = bchalo_ref[...].astype(F32)
    done = convolved(windows.at[tiles], bc_ref[...], kbc_ref[...])
    bmat_ref[...] = done
    for start in range(0, done.shape[0], CH):
        part = done[start : start + CH].astype(F32).T
        trans[:, start : start + CH] = part.astype(BF16)
    rows = state.shape[0] // len(pieces)
    xhalo = xhalo_ref[...].astype(F32)
    for begin in range(0, width, 256):
        loads = []
        for start in (begin, begin + LANES):
            at = slice(start, start + LANES)
            window = windows.at[start // LANES]
            window[8 - halo : 8, :] = xhalo[:, at]
            done = convolved(window, x_ref[:, at], kx_ref[:, at])
            xc_ref[:, at] = done
            loads.append((done.astype(F32) * dot(loads_ref[...], spread[:, at])).astype(BF16))
        at = slice(begin, begin + 256)
        state[:, at] = dot(trans[...], jnp.concatenate(loads, axis=1))
    for k, piece in enumerate(pieces):
        owner = me_ref[0] ^ k
        take = state[pl.ds(pl.multiple_of(owner * rows, rows), rows), :]
        piece[:, :width] = take.astype(BF16)
        piece[:, width:] = jnp.broadcast_to(final_ref[0:1, :], (rows, LANES)).astype(BF16)


def prefix_kernel(me_ref, spread, *rest, groups):
    size = len(rest) - 5
    pieces = rest[:size]
    part_ref, gain_ref, out_ref, states, decays = rest[size:]
    rows, width = out_ref.shape
    span = width // groups
    for step, piece in enumerate(pieces):
        owner = me_ref[0] ^ step
        for group in range(groups):
            start = group * (span + LANES)
            at = slice(group * span, (group + 1) * span)
            states[owner, :, at] = piece[:, start : start + span].astype(F32)
        decays[owner] = piece[:, span : span + LANES].astype(F32)
    held = jnp.zeros((rows, width), F32)
    gain = jnp.ones((1, width), F32)
    for shard in range(size):
        part_ref[shard] = held
        gain_ref[shard] = gain
        factor = dot(decays[shard, :, : spread.shape[0]].astype(BF16), spread[...])[0:1]
        held = factor * held + states[shard]
        gain = factor * gain
    out_ref[...] = held.astype(BF16)


def enter_kernel(me_ref, part_ref, gain_ref, low_ref, *outs):
    low = low_ref[...].astype(F32)
    for step, out in enumerate(outs):
        owner = me_ref[0] ^ step
        out[...] = (part_ref[owner] + gain_ref[owner] * low).astype(BF16)


def inner_kernel(
    xc_ref,
    bmat_ref,
    c_ref,
    chalo_ref,
    kc_ref,
    cum_ref,
    row_ref,
    grown_ref,
    whole_ref,
    tails_ref,
    decay_ref,
    z_ref,
    skips_ref,
    spread,
    y_ref,
    p_ref,
    cmat_ref,
    window,
    carry,
    *,
    head_size,
    first,
    heads,
):
    width = xc_ref.shape[1]
    halo = chalo_ref.shape[0]

    @pl.when(pl.program_id(0) == 0)
    def _():
        window[8 - halo : 8, :] = chalo_ref[...].astype(F32)
        carry[...] = jnp.zeros_like(carry)

    for sub in range(xc_ref.shape[0] // CH):
        here = slice(sub * CH, (sub + 1) * CH)
        block = pl.program_id(0) * (xc_ref.shape[0] // CH) + sub
        cmat = convolved(window, c_ref[here, :], kc_ref[...])
        window[:8, :] = window[CH : CH + 8, :]
        cmat_ref[here, :] = cmat
        bmat = bmat_ref[here, :]
        trans = bmat.astype(F32).T.astype(BF16)
        cum = pltpu.roll(cum_ref[...], LANES - block * heads, 1)
        grown = packed(grown_ref[...], block * heads, heads)
        whole = packed(whole_ref[...], block * heads, heads)
        tails = packed(tails_ref[...], block * heads, heads)
        r = lax.broadcasted_iota(jnp.int32, (CH, CH), 0)
        c = lax.broadcasted_iota(jnp.int32, (CH, CH), 1)
        left = c < head_size
        per_tile = LANES // head_size
        pairs = jnp.where(r >= c, dot_rows(cmat, bmat), 0.0)
        for tile in range(width // LANES):
            at = slice(tile * LANES, (tile + 1) * LANES)
            xc = xc_ref[here, at]
            weights = []
            for head in range(first + tile * per_tile, first + (tile + 1) * per_tile):
                gap = cum[:, head : head + 1] - row_ref[sub * heads + head : sub * heads + head + 1, :]
                weights.append((pairs * jnp.exp(jnp.minimum(gap, 60.0))).astype(BF16))
            zero = jnp.zeros_like(xc)
            stacked = [jnp.where(left, xc, zero), jnp.where(left, zero, xc)]
            y = dot(jnp.concatenate(weights, axis=1), jnp.concatenate(stacked, axis=0))
            before = carry[:, at]
            y = y + dot(grown, spread[:, at]) * dot(cmat, before.astype(BF16))
            load = (xc.astype(F32) * dot(tails, spread[:, at])).astype(BF16)
            carry[:, at] = decay_ref[sub, :, at] * before + dot(trans, load)
            y = y + skips_ref[:, at] * xc.astype(F32)
            gate = silu(z_ref[here, at].astype(F32))
            y_ref[here, at] = y * gate
            p_ref[here, at] = (gate * dot(whole, spread[:, at])).astype(BF16)


def mix_kernel(me_ref, y_ref, p_ref, cmat_ref, gain_ref, weight_ref, ids_ref, *rest, size, chained, final):
    pieces, rest = rest[:size], rest[size:]
    if chained:
        before_ref, rest = rest[0], rest[1:]
    mixed_ref, out_ref, wide, enter, gated, acc = rest
    block = pl.program_id(0)
    count, width = y_ref.shape
    rows = wide.shape[0] // size

    @pl.when(block == 0)
    def _():
        for step, piece in enumerate(pieces):
            owner = me_ref[0] ^ step
            wide[pl.ds(pl.multiple_of(owner * rows, rows), rows), :] = piece[...].astype(F32)
        enter[...] = wide[...].astype(BF16)
        acc[...] = before_ref[...] if chained else jnp.zeros_like(acc)

    cmat = cmat_ref[...]
    square = jnp.zeros((count, LANES), F32)
    for start in range(0, width, LANES):
        at = slice(start, start + LANES)
        g = y_ref[:, at] + p_ref[:, at].astype(F32) * dot(cmat, enter[:, at])
        gated[:, at] = g
        square = square + g * g
    scale = lax.rsqrt(jnp.sum(square, axis=1, keepdims=True) / width + EPS)
    scale = jnp.broadcast_to(scale, (count, LANES))
    read = jnp.zeros((count, LANES), F32)
    for start in range(0, width, LANES):
        at = slice(start, start + LANES)
        mixed = (gated[:, at] * scale * gain_ref[:, at].astype(F32)).astype(BF16)
        mixed_ref[:, at] = mixed
        read = read + mixed.astype(F32) * weight_ref[:, at].astype(F32)
    labels = lax.broadcasted_iota(jnp.int32, (LANES, count), 0)
    member = jnp.where(labels == ids_ref[0], 1.0, 0.0).astype(BF16)
    read = jnp.broadcast_to(jnp.sum(read, axis=1, keepdims=True), (count, LANES))
    high = read.astype(BF16).astype(F32)
    middle = (read - high).astype(BF16).astype(F32)
    lane = lax.broadcasted_iota(jnp.int32, (count, LANES), 1)
    terms = jnp.where(lane == 0, high, jnp.where(lane == 1, middle, read - high - middle))
    one = 1.0 if final else 0.0
    terms = jnp.where(lane == 3, one, jnp.where(lane > 3, 0.0, terms)).astype(BF16)
    acc[...] += dot(member, terms)

    @pl.when(block == pl.num_programs(0) - 1)
    def _():
        if final:
            flat = acc[...].T
            sums = flat[0:1] + flat[1:2] + flat[2:3]
            both = jnp.concatenate([sums, flat[3:4]], axis=0)
            out_ref[...] = jnp.broadcast_to(both[None], out_ref.shape)
        else:
            out_ref[...] = acc[...]


def flush_kernel(*refs):
    parts, out_ref, sems = refs[:-2], refs[-2], refs[-1]
    span = out_ref.shape[1] // len(parts)
    copies = [
        pltpu.make_async_copy(part, out_ref.at[:, k * span : (k + 1) * span], sems.at[k])
        for k, part in enumerate(parts)
    ]
    for copy in copies:
        copy.start()
    for copy in copies:
        copy.wait()


def loss_kernel(parts_ref, ids_ref, logits_ref, order_ref, grad_ref, loss_ref, *, copies, total):
    both = jnp.sum(parts_ref[...], axis=0)
    lane = lax.broadcasted_iota(jnp.int32, (1, LANES), 1)
    valid = lane < NP
    sums = both[0:1]
    counts = jnp.where(valid, both[1:2] / copies, 1.0)
    squash = jnp.tanh(sums / counts / CAP)
    scores = CAP * squash
    student = scores - jnp.log(jnp.sum(jnp.where(valid, jnp.exp(scores), 0.0)))
    hit = order_ref[...] == lax.broadcasted_iota(jnp.int32, (NP, LANES), 1)
    teacher = jnp.sum(jnp.where(hit, logits_ref[...], 0.0), axis=0, keepdims=True)
    teacher = teacher - jnp.log(jnp.sum(jnp.where(valid, jnp.exp(teacher), 0.0)))
    chance = jnp.where(valid, jnp.exp(teacher), 0.0)
    loss_ref[0, 0] = jnp.sum(chance * (teacher - student))
    coef = (jnp.exp(student) - chance) * (1.0 - squash * squash) * total / counts
    coef = jnp.broadcast_to(jnp.where(valid, coef, 0.0), (LANES, LANES)).T
    label = lax.broadcasted_iota(jnp.int32, (LANES, LANES), 0)
    for block in range(ids_ref.shape[0]):
        picked = jnp.where(label == ids_ref[block], coef, 0.0)
        grad_ref[block : block + 1, :] = jnp.sum(picked, axis=0, keepdims=True)


def swapped(pieces, axis):
    count = lax.axis_size(axis)
    out = [pieces[0]]
    for step in range(1, len(pieces)):
        route = [(i, i ^ step) for i in range(count)]
        out.append(lax.ppermute(pieces[step], axis, route))
    return out


def per_device(
    x_in,
    z_in,
    bc_in,
    dt_raw,
    dt_bias,
    a_log,
    conv_x,
    conv_bc,
    skip_gain,
    norm_gain,
    score_weight,
    passage_ids,
    teacher_logits,
    teacher_order,
):
    taps = conv_x.shape[0]
    count, width = x_in.shape
    groups = bc_in.shape[1]
    state_size = bc_in.shape[3]
    heads = dt_raw.shape[1] // groups
    span = width // groups
    head_size = span // heads
    pair = 2 * state_size
    blocks = count // CH
    shards = lax.axis_size("seq")
    columns = lax.axis_size("head")
    half = shards // 2
    rows = state_size // half
    bc = bc_in.reshape(count, -1)
    me = lax.axis_index("seq").astype(jnp.int32).reshape(1) % half
    ahead = [(i, i + 1) for i in range(shards - 1)]
    edge = jnp.concatenate([x_in[count - taps + 1 :], bc[count - taps + 1 :]], axis=1)
    halo = lax.ppermute(edge, "seq", ahead)
    ids = passage_ids.reshape(blocks, 1, CH)
    x_in, bc = lax.optimization_barrier((x_in, bc))

    smem = pl.BlockSpec(memory_space=pltpu.SMEM)
    vmem = pl.BlockSpec(memory_space=pltpu.VMEM)

    def block_of(shape, *index):
        return pl.BlockSpec(shape, lambda i: tuple(i if k is None else k for k in index))

    def hbm(array):
        return pltpu.with_memory_space_constraint(array, pltpu.HBM)

    def shaped(dtype, *shape):
        return jax.ShapeDtypeStruct(shape, dtype)

    def cost(flops, moved, steps=0):
        return pl.CostEstimate(flops=flops, bytes_accessed=moved, transcendentals=steps)

    params = pltpu.CompilerParams(
        dimension_semantics=("arbitrary",), vmem_limit_bytes=VMEM_LIMIT
    )
    plain = pltpu.CompilerParams(vmem_limit_bytes=VMEM_LIMIT)
    somewhere = pl.BlockSpec(memory_space=pl.ANY)
    every = groups * heads
    prepared = [
        shaped(F32, taps, width),
        shaped(F32, taps, groups * pair),
        shaped(BF16, 2 * every, width),
        shaped(F32, CH, LANES),
        shaped(F32, blocks * every, CH),
        shaped(F32, CH, LANES),
        shaped(F32, CH, LANES),
        shaped(F32, CH, LANES),
        shaped(BF16, count, 2 * every),
        shaped(F32, blocks, 1, width),
        shaped(F32, 8, LANES),
        shaped(F32, 1, width),
    ]
    (kx, kbc, spread, cum, rowed, grown, whole, tails, loads, decay, final, skips) = pl.pallas_call(
        partial(prep_kernel, head_size=head_size),
        name="prep",
        grid=(1,),
        in_specs=[somewhere] * 6,
        out_specs=[block_of(out.shape, *(0 for _ in out.shape)) for out in prepared],
        out_shape=prepared,
        scratch_shapes=[
            pltpu.VMEM((every, count), F32),
            pltpu.VMEM(conv_x.shape, BF16),
            pltpu.VMEM(conv_bc.shape, BF16),
            pltpu.VMEM((1, every), F32),
            pltpu.VMEM((1, every), F32),
            pltpu.VMEM((1, every), F32),
            pltpu.SemaphoreType.DMA((6,)),
        ],
        compiler_params=params,
        cost_estimate=cost(10**9, 4 * 10**6, 10**5),
    )(
        hbm(dt_raw.T),
        hbm(conv_x),
        hbm(conv_bc),
        hbm(dt_bias[None]),
        hbm(a_log[None]),
        hbm(skip_gain[None]),
    )

    def states(group, pieces):
        return pl.pallas_call(
            partial(state_kernel, passed=len(pieces)),
            name="state%d" % group,
            grid=(1,),
            in_specs=[
                smem,
                block_of((count, span), 0, group),
                block_of((taps - 1, span), 0, group),
                block_of((count, LANES), 0, 2 * group),
                block_of((taps - 1, LANES), 0, width // LANES + 2 * group),
                block_of((count, 2 * every), 0, 0),
                block_of((8, LANES), 0, 0),
                block_of((taps, span), 0, group),
                block_of((taps, LANES), 0, 2 * group),
                block_of((2 * every, span), 0, group),
            ]
            + [somewhere] * len(pieces),
            out_specs=[block_of((count, span), 0, 0), block_of((count, LANES), 0, 0)]
            + [block_of((rows, span + LANES), 0, group)] * half,
            out_shape=[shaped(BF16, count, span), shaped(BF16, count, LANES)]
            + [shaped(BF16, rows, groups * (span + LANES))] * half,
            scratch_shapes=[
                pltpu.VMEM((span // LANES + 1, 8 + count, LANES), F32),
                pltpu.VMEM((state_size, count), BF16),
                pltpu.VMEM((state_size, span), F32),
            ],
            input_output_aliases={10 + k: 2 + k for k in range(len(pieces))},
            compiler_params=params,
            cost_estimate=cost(10**9, 4 * 10**6, 10**6),
        )(
            me,
            x_in,
            halo,
            bc,
            halo,
            loads,
            final,
            kx,
            kbc,
            spread,
            *pieces,
        )

    def prefix(arrived):
        return pl.pallas_call(
            partial(prefix_kernel, groups=groups),
            name="prefix",
            grid=(1,),
            in_specs=[smem, block_of((2 * every, width), 0, 0)]
            + [block_of((rows, groups * (span + LANES)), 0, 0)] * half,
            out_specs=[
                block_of((half, rows, width), 0, 0, 0),
                block_of((half, 1, width), 0, 0, 0),
                block_of((rows, width), 0, 0),
            ],
            out_shape=[
                shaped(F32, half, rows, width),
                shaped(F32, half, 1, width),
                shaped(BF16, rows, width),
            ],
            scratch_shapes=[
                pltpu.VMEM((half, rows, width), F32),
                pltpu.VMEM((half, rows, LANES), F32),
            ],
            compiler_params=params,
            cost_estimate=cost(10**6, 10**6),
        )(me, spread, *arrived)

    def enter(part, gain, low):
        return pl.pallas_call(
            enter_kernel,
            name="enter",
            in_specs=[smem] + [vmem] * 3,
            out_specs=[vmem] * half,
            out_shape=[shaped(BF16, rows, width)] * half,
            compiler_params=plain,
            cost_estimate=cost(10**6, 10**6),
        )(me, part, gain, low)

    def inner(group, xc, bmat):
        return pl.pallas_call(
            partial(inner_kernel, head_size=head_size, first=group * heads, heads=every),
            name="inner%d" % group,
            grid=(blocks // 2,),
            in_specs=[
                block_of((2 * CH, span), None, 0),
                block_of((2 * CH, LANES), None, 0),
                block_of((2 * CH, LANES), None, 2 * group + 1),
                block_of((taps - 1, LANES), 0, width // LANES + 2 * group + 1),
                block_of((taps, LANES), 0, 2 * group + 1),
                block_of((CH, LANES), 0, 0),
                block_of((2 * every, CH), None, 0),
                block_of((CH, LANES), 0, 0),
                block_of((CH, LANES), 0, 0),
                block_of((CH, LANES), 0, 0),
                block_of((2, 1, span), None, 0, group),
                block_of((2 * CH, span), None, group),
                block_of((1, span), 0, group),
                block_of((2 * every, span), 0, group),
            ],
            out_specs=[block_of((2 * CH, span), None, 0)] * 2 + [block_of((2 * CH, LANES), None, 0)],
            out_shape=[
                shaped(F32, count, span),
                shaped(BF16, count, span),
                shaped(BF16, count, LANES),
            ],
            scratch_shapes=[
                pltpu.VMEM((8 + CH, LANES), F32),
                pltpu.VMEM((state_size, span), F32),
            ],
            compiler_params=params,
            cost_estimate=cost(2 * 10**9, 10**7, 2 * 10**6),
        )(
            xc,
            bmat,
            bc,
            halo,
            kbc,
            cum,
            rowed,
            grown,
            whole,
            tails,
            decay,
            z_in,
            skips,
            spread,
        )

    mix_rows = MIX_BLOCKS * CH

    def mix(group, y, p, cmat, entering, before):
        final = group == groups - 1
        copies = shards * columns
        sent = (copies, 2, LANES) if final else (LANES, LANES)
        chained = before is not None
        extra = [block_of((LANES, LANES), 0, 0)]
        return pl.pallas_call(
            partial(mix_kernel, size=half, chained=chained, final=final),
            name="mix%d" % group,
            grid=(count // mix_rows,),
            in_specs=[
                smem,
                block_of((mix_rows, span), None, 0),
                block_of((mix_rows, span), None, 0),
                block_of((mix_rows, LANES), None, 0),
                block_of((1, span), 0, group),
                block_of((1, span), 0, group),
                block_of((1, 1, mix_rows), None, 0, 0),
            ]
            + [block_of((rows, span), 0, group)] * half
            + (extra if chained else []),
            out_specs=[block_of((mix_rows, span), None, 0), block_of(sent, *(0 for _ in sent))],
            out_shape=[shaped(BF16, count, span), shaped(F32, *sent)],
            scratch_shapes=[
                pltpu.VMEM((state_size, span), F32),
                pltpu.VMEM((state_size, span), BF16),
                pltpu.VMEM((mix_rows, span), F32),
                pltpu.VMEM((LANES, LANES), F32),
            ],
            compiler_params=params,
            cost_estimate=cost(5 * 10**8, 5 * 10**6),
        )(me, y, p, cmat, norm_gain[None], score_weight[None], passage_ids.reshape(-1, 1, mix_rows), *entering, *([before] if chained else []))

    lower = [(i, i + half) for i in range(half)]
    local, pieces = [], []
    for group in range(groups):
        local.append(states(group, pieces))
        pieces = local[-1][2:]
    within = [inner(group, *local[group][:2]) for group in range(groups)]
    arrived = swapped(pieces, "seq")
    *arrived, y = lax.optimization_barrier((*arrived, within[0][0]))
    within[0] = (y, *within[0][1:])
    part, gain, low = prefix(arrived)
    low = lax.ppermute(low, "seq", lower)
    if groups > 1:
        low, y = lax.optimization_barrier((low, within[1][0]))
        within[1] = (y, *within[1][1:])
    entering = swapped(enter(part, gain, low), "seq")
    sent, mixed = None, []
    for group in range(groups):
        done, sent = mix(group, *within[group], entering, sent)
        mixed.append(done)

    shared = lax.all_to_all(sent, ("seq", "head"), split_axis=0, concat_axis=0, tiled=True)
    mixed_out = pl.pallas_call(
        flush_kernel,
        name="flush",
        in_specs=[somewhere] * groups,
        out_specs=somewhere,
        out_shape=shaped(BF16, count, width),
        scratch_shapes=[pltpu.SemaphoreType.DMA((groups,))],
        compiler_params=plain,
        cost_estimate=cost(0, 4 * 10**6),
    )(*mixed)
    grad, loss = pl.pallas_call(
        partial(loss_kernel, copies=columns, total=shards * count),
        name="loss",
        in_specs=[vmem] * 4,
        out_specs=[vmem, smem],
        out_shape=[shaped(F32, blocks, LANES), shaped(F32, 1, 1)],
        compiler_params=plain,
    )(shared, ids, teacher_logits[:, None], teacher_order[:, None])
    return (mixed_out, grad.reshape(count), loss.reshape(()))


def solution(mesh):
    placed = (
        P("seq", "head"),
        P("seq", "head"),
        P("seq", "head", None, None),
        P("seq", "head"),
        P("head"),
        P("head"),
        P(None, "head"),
        P(None, "head", None, None),
        P("head"),
        P("head"),
        P("head"),
        P("seq"),
        P(),
        P(),
    )
    return jax.shard_map(
        per_device,
        mesh=mesh,
        in_specs=placed,
        out_specs=(P("seq", "head"), P("seq"), P()),
        check_vma=False,
    )
```
